32 devices in a mesh: seq: 4 (over y, x), dp: 8 (over z, core).
Axes of the slice: x: 2, y: 2, z: 4, core: 2. Of those that a mesh axis runs over, the one named last changes fastest.
Arguments:
- hidden_in: bfloat16 [24, 512, 768], P('dp', 'seq'), may hold values from -6 to 6
- lengths: int32 [24], P('dp'), may hold values from 20 to 512, as said below
- qkv_weight: bfloat16 [768, 2304], replicated, may hold values from -0.21875 to 0.21875
- query_bias: float32 [768], replicated, may hold values from -3 to 3
- value_bias: float32 [768], replicated, may hold values from -0.6 to 0.6
- out_weight: bfloat16 [768, 768], replicated, may hold values from -1.75 to 1.75
- out_bias: float32 [768], replicated, may hold values from -1.2 to 1.2
- attn_gain: float32 [768], replicated, may hold values from 0.5 to 1.5
- attn_shift: float32 [768], replicated, may hold values from -1.2 to 1.2
- up_weight: bfloat16 [768, 3072], replicated, may hold values from -0.21875 to 0.21875
- up_bias: float32 [3072], replicated, may hold values from -3 to 3
- down_weight: bfloat16 [3072, 768], replicated, may hold values from -0.109375 to 0.109375
- down_bias: float32 [768], replicated, may hold values from -1.2 to 1.2
- ffn_gain: float32 [768], replicated, may hold values from 0.5 to 1.5
- ffn_shift: float32 [768], replicated, may hold values from -1.2 to 1.2
- cotangent: bfloat16 [24, 512, 768], P('dp', 'seq'), may hold values from -6 to 6
Outputs:
- layer_out: bfloat16 [24, 512, 768], P('dp', 'seq')
- input_grad: bfloat16 [24, 512, 768], P('dp', 'seq')
- qkv_weight_grad: float32 [768, 2304], replicated
- query_bias_grad: float32 [768], replicated
- value_bias_grad: float32 [768], replicated
- out_weight_grad: float32 [768, 768], replicated
- out_bias_grad: float32 [768], replicated
- attn_gain_grad: float32 [768], replicated
- attn_shift_grad: float32 [768], replicated
- up_weight_grad: float32 [768, 3072], replicated
- up_bias_grad: float32 [3072], replicated
- down_weight_grad: float32 [3072, 768], replicated
- down_bias_grad: float32 [768], replicated
- ffn_gain_grad: float32 [768], replicated
- ffn_shift_grad: float32 [768], replicated
The draws below stay inside these ranges and needn't reach their ends.
Inputs may be any that keep to these rules, and one draw needn't show every extreme that they name: `lengths`: keys at positions at or past a passage's length are padding; in every draw some passage has length 512 and some 20.
All inputs are finite; a program needn't handle non-finite values.
Results may differ from the reference program's by a relative error of at most 0.015.
Values may be sent and summed in bfloat16 or wider, within the bound.
No kernel may reach another device: no remote copies, remote signals or barrier semaphores. Data moves between devices by JAX's collectives and lax.ppermute only.
A program may use at most 192 MiB of HBM per device.

```python
import jax
import jax.numpy as jnp
from jax import lax

D = 768
HEADS = 12
HEAD = 64
FF = 3072
LEN = 512
MINLEN = 20
PASSAGES = 24


def draw_lengths(key, part):
    first_key, second_key, third_key = jax.random.split(key, 3)
    values = jax.random.randint(first_key, (PASSAGES,), MINLEN, LEN + 1)
    longest = jax.random.randint(second_key, (), 0, PASSAGES)
    shortest = (longest + 1 + jax.random.randint(third_key, (), 0, PASSAGES - 1)) % PASSAGES
    values = values.at[longest].set(LEN).at[shortest].set(MINLEN)
    return values.astype(jnp.int32)


def levels(stream_key, dims, pieces, low, high):
    level, own = 1.0, jax.random.fold_in(stream_key, 6)
    for dim, shards_of in pieces:
        heights = jnp.exp(jax.random.uniform(jax.random.fold_in(own, dim), (shards_of,), jnp.float32, low / len(pieces), high / len(pieces)))
        level = level * jnp.repeat(heights, dims[dim] // shards_of).reshape([-1 if axis == dim else 1 for axis in range(len(dims))])
    return level


def bell_draw(own_key, extent, deviation, most, cuts=(), dtype=jnp.bfloat16):
    level = levels(own_key, extent, cuts, -0.22, 0.18) if cuts else 1.0
    values = jax.random.normal(own_key, extent, jnp.float32) * deviation * level
    return jnp.minimum(jnp.maximum(values, -most), most).astype(dtype)


def setup_inputs(seed: int = 0) -> dict:
    streams_of = jax.random.split(jax.random.key(seed), 17)
    hidden_in = bell_draw(streams_of[0], (PASSAGES, LEN, D), 1.0, 6.0, ((0, 8), (1, 4)))
    lengths = draw_lengths(jax.random.fold_in(streams_of[16], 71), 0)
    qkv_weight = bell_draw(streams_of[2], (D, 3 * D), D ** -0.5, 0.21875)
    query_bias = bell_draw(streams_of[3], (D,), 0.5, 3.0, (), jnp.float32)
    value_bias = bell_draw(streams_of[4], (D,), 0.1, 0.6, (), jnp.float32)
    out_weight = bell_draw(streams_of[5], (D, D), (max(D // 64, 4)) ** -0.5, 1.75)
    out_bias = bell_draw(streams_of[6], (D,), 0.2, 1.2, (), jnp.float32)
    attn_gain = jnp.clip(1.0 + 0.1 * jax.random.normal(streams_of[7], (D,), jnp.float32), 0.5, 1.5)
    attn_shift = bell_draw(streams_of[8], (D,), 0.2, 1.2, (), jnp.float32)
    up_weight = bell_draw(streams_of[9], (D, FF), D ** -0.5, 0.21875)
    up_bias = bell_draw(streams_of[10], (FF,), 0.5, 3.0, (), jnp.float32)
    down_weight = bell_draw(streams_of[11], (FF, D), FF ** -0.5, 0.109375)
    down_bias = bell_draw(streams_of[12], (D,), 0.2, 1.2, (), jnp.float32)
    ffn_gain = jnp.clip(1.0 + 0.1 * jax.random.normal(streams_of[13], (D,), jnp.float32), 0.5, 1.5)
    ffn_shift = bell_draw(streams_of[14], (D,), 0.2, 1.2, (), jnp.float32)
    cotangent = bell_draw(streams_of[15], (PASSAGES, LEN, D), 1.0, 6.0, ((0, 8), (1, 4)))
    return dict(hidden_in=hidden_in, lengths=lengths, qkv_weight=qkv_weight, query_bias=query_bias, value_bias=value_bias, out_weight=out_weight, out_bias=out_bias, attn_gain=attn_gain, attn_shift=attn_shift, up_weight=up_weight, up_bias=up_bias, down_weight=down_weight, down_bias=down_bias, ffn_gain=ffn_gain, ffn_shift=ffn_shift, cotangent=cotangent)


@jax.custom_vjp
def low(v):
    return lax.optimization_barrier(v.astype(jnp.bfloat16)).astype(jnp.float32)

@jax.custom_vjp
def low_back(v):
    return v

def low_keep(v):
    return (low(v), None)

def low_pass(kept, grad):
    return (grad,)

def back_keep(v):
    return (v, None)

def back_low(kept, grad):
    return (low(grad),)
low.defvjp(low_keep, low_pass)
low_back.defvjp(back_keep, back_low)

def layer_norm(values, gain, shift):
    center = values - lax.optimization_barrier(jnp.mean(values, -1, keepdims=True))
    spread = lax.optimization_barrier(jnp.mean(center * center, -1, keepdims=True))
    return center * lax.rsqrt(spread + 1e-12) * gain + shift

def mult(left, right):
    return jnp.dot(left, right, precision=lax.Precision.HIGHEST)

def passage(item):
    query, keys, values, length = item
    raw = jnp.einsum('qhd,khd->hqk', query, keys, precision=lax.Precision.HIGHEST) * HEAD ** (-0.5)
    scores = low_back(raw)
    valid = jnp.arange(LEN) < length
    scores = jnp.where(valid[None, None, :], scores, -1e+30)
    probs = jax.nn.softmax(scores, axis=-1)
    return jnp.einsum('hqk,khd->qhd', low(probs), values, precision=lax.Precision.HIGHEST)

def forward(tokens, lengths, qkv_weight, query_bias, value_bias, out_weight, out_bias, attn_gain, attn_shift, up_weight, up_bias, down_weight, down_bias, ffn_gain, ffn_shift):
    rows = tokens.reshape(PASSAGES * LEN, D)
    joined = jnp.concatenate([query_bias, jnp.zeros_like(query_bias), value_bias])
    qkv = low(low_back(mult(rows, qkv_weight) + joined))
    qkv = qkv.reshape(PASSAGES, LEN, 3, HEADS, HEAD)
    context = lax.map(jax.checkpoint(passage), (qkv[:, :, 0], qkv[:, :, 1], qkv[:, :, 2], lengths))
    context = low(low_back(context)).reshape(PASSAGES * LEN, D)
    attn = low_back(mult(context, out_weight) + out_bias)
    first = layer_norm(rows + attn, attn_gain, attn_shift)
    upper = low_back(mult(low(first), up_weight) + up_bias)
    active = low(jax.nn.gelu(upper, approximate=False))
    ffn = low_back(mult(active, down_weight) + down_bias)
    result = layer_norm(first + ffn, ffn_gain, ffn_shift)
    return result.reshape(PASSAGES, LEN, D)

def reference(hidden_in, lengths, qkv_weight, query_bias, value_bias, out_weight, out_bias, attn_gain, attn_shift, up_weight, up_bias, down_weight, down_bias, ffn_gain, ffn_shift, cotangent):
    floats = [hidden_in, qkv_weight, query_bias, value_bias, out_weight, out_bias, attn_gain, attn_shift, up_weight, up_bias, down_weight, down_bias, ffn_gain, ffn_shift]
    floats = [item.astype(jnp.float32) for item in floats]

    def closed(tokens, *weights):
        return forward(tokens, lengths, *weights)
    result, pullback = jax.vjp(closed, *floats)
    grads = pullback(cotangent.astype(jnp.float32))
    return (result.astype(jnp.bfloat16), grads[0].astype(jnp.bfloat16), grads[1], grads[2], grads[3], grads[4], grads[5], grads[6], grads[7], grads[8], grads[9], grads[10], grads[11], grads[12], grads[13])
```

```python
import functools
import math

import jax
import jax.numpy as jnp
from jax import lax
from jax.experimental import pallas as pl
from jax.experimental.pallas import tpu as pltpu
from jax.sharding import PartitionSpec as P

HEADS = 12
EPS = 1e-12
BF = jnp.bfloat16
F32 = jnp.float32
VMEM_LIMIT = 60 * 1024 * 1024
LOG2E = math.log2(math.e)
S_SEQ, S_LEN, S_CORE, S_X, S_Y = range(5)


def dot_nn(left, right):
    return lax.dot_general(left, right, (((1,), (0,)), ((), ())), preferred_element_type=F32)


def dot_nt(left, right):
    return lax.dot_general(left, right, (((1,), (1,)), ((), ())), preferred_element_type=F32)


def dot_tn(left, right):
    return lax.dot_general(left, right, (((0,), (0,)), ((), ())), preferred_element_type=F32)


def params(flag=None):
    return pltpu.CompilerParams(vmem_limit_bytes=VMEM_LIMIT)


def cost(flops, nbytes, trans=0):
    return pl.CostEstimate(flops=int(flops), bytes_accessed=int(nbytes), transcendentals=int(trans))


def full(shape):
    zeros = (0,) * len(shape)
    return pl.BlockSpec(shape, lambda *_: zeros)


def shape_of(shape, dtype):
    return jax.ShapeDtypeStruct(shape, dtype)


def attn_fwd_body(sc, h0, h1, h2, h3, wq, wk, wv, qb, vb, wo, ob, gain, shift,
                  hid, q_o, k_o, v_o, ctx_o, lse_o, n1_o, r1_o, low_o, acc, lse_s):
    step = pl.program_id(0)
    steps = pl.num_programs(0)
    local = h0.shape[0]
    rows = hid.shape[0]
    head = wq.shape[1] // 2

    @pl.when(step == 0)
    def _():
        for at, ref in enumerate((h0, h1, h2, h3)):
            hid[at * local:(at + 1) * local, :] = ref[...]
        acc[...] = jnp.zeros_like(acc)
        lse_s[...] = jnp.zeros_like(lse_s)

    x = hid[...]
    w = jnp.concatenate([wq[...], wk[...], wv[...]], axis=1)
    both = dot_nn(x, w)
    wide = 2 * head
    q_o[...] = (both[:, :wide] + qb[...]).astype(BF)
    k_o[...] = both[:, wide:2 * wide].astype(BF)
    v_o[...] = (both[:, 2 * wide:] + vb[...]).astype(BF)
    k = k_o[...]
    v = v_o[...]
    key = lax.broadcasted_iota(jnp.int32, (1, rows), 1)
    place = ((key // local) ^ sc[S_SEQ]) * local + key % local
    mask = jnp.where(place < sc[S_LEN], 0.0, -1e30).astype(F32)
    scale = head ** (-0.5) * LOG2E
    chunk = 256
    lane = lax.broadcasted_iota(jnp.int32, (chunk, wide), 1)
    lane_l = lax.broadcasted_iota(jnp.int32, (chunk, lse_s.shape[1]), 1)
    for part in range(rows // chunk):
        span = pl.ds(part * chunk, chunk)
        q = q_o[span, :]
        outs = []
        tops = []
        for h in range(2):
            mine = (lane >= h * head) & (lane < (h + 1) * head)
            qh = jnp.where(mine, q, jnp.zeros_like(q))
            s = dot_nt(qh, k) * scale + mask
            top = jnp.max(s, -1, keepdims=True)
            e = jnp.exp2(s - top)
            total = jnp.sum(e, -1, keepdims=True)
            pv = dot_nn(e.astype(BF), v)
            outs.append(pv / total)
            tops.append(top + jnp.log2(total))
        ctx_o[span, :] = jnp.where(lane < head, outs[0], outs[1]).astype(BF)
        old = lse_s[span, :]
        old = jnp.where(lane_l == 2 * step, tops[0], old)
        lse_s[span, :] = jnp.where(lane_l == 2 * step + 1, tops[1], old)
    acc[...] += dot_nn(ctx_o[...], wo[...])

    @pl.when(step == steps - 1)
    def _():
        lse_o[...] = jnp.transpose(lse_s[...])[:lse_o.shape[0], :]
        for part in range(rows // local):
            span = pl.ds(part * local, local)
            val = hid[span, :].astype(F32) + (acc[span, :] + ob[...])
            cen = val - jnp.mean(val, -1, keepdims=True)
            r = lax.rsqrt(jnp.mean(cen * cen, -1, keepdims=True) + EPS)
            n = cen * r
            n1_o[span, :] = n
            r1_o[span, :] = jnp.broadcast_to(r, (local, r1_o.shape[1]))
            low_o[span, :] = (n * gain[...] + shift[...]).astype(BF)


def attn_fwd(sc, blocks, qkv_w, qb, vb, out_w, ob, gain, shift):
    local, width = blocks[0].shape
    rows = local * len(blocks)
    pairs = HEADS // 2
    wide = width // pairs
    row = lambda i, s: (0, i)
    grid = pltpu.PrefetchScalarGridSpec(
        num_scalar_prefetch=1,
        grid=(pairs,),
        in_specs=[full((local, width))] * 4 + [
            pl.BlockSpec((width, wide), lambda i, s: (0, i)),
            pl.BlockSpec((width, wide), lambda i, s: (0, pairs + i)),
            pl.BlockSpec((width, wide), lambda i, s: (0, 2 * pairs + i)),
            pl.BlockSpec((1, wide), row),
            pl.BlockSpec((1, wide), row),
            pl.BlockSpec((wide, width), lambda i, s: (i, 0)),
            full((1, width)), full((1, width)), full((1, width)),
        ],
        out_specs=[
            full((rows, width)),
            pl.BlockSpec((rows, wide), row),
            pl.BlockSpec((rows, wide), row),
            pl.BlockSpec((rows, wide), row),
            pl.BlockSpec((rows, wide), row),
            full((16, rows)),
            full((rows, width)),
            full((rows, 128)),
            full((rows, width)),
        ],
        scratch_shapes=[pltpu.VMEM((rows, width), F32), pltpu.VMEM((rows, 128), F32)],
    )
    wide_bf = shape_of((rows, width), BF)
    return pl.pallas_call(
        attn_fwd_body,
        grid_spec=grid,
        out_shape=[wide_bf, wide_bf, wide_bf, wide_bf, wide_bf, shape_of((16, rows), F32),
                   shape_of((rows, width), F32), shape_of((rows, 128), F32), wide_bf],
        compiler_params=params(),
        cost_estimate=cost(2 * rows * width * width * 4 + 4 * rows * rows * width, 12 * rows * width + 8 * width * width,
                           HEADS * rows * rows),
        name="attn_fwd",
    )(sc, *blocks, qkv_w, qkv_w, qkv_w, qb, vb, out_w, ob, gain, shift)


def ffn_fwd_body(low, n1, gain1, shift1, wu, ub, wd, db, gain2, shift2, c0, c1, c2, c3,
                 act_o, slope_o, l0, l1, l2, l3, dsec_o, dffn_o, stat_o, acc):
    step = pl.program_id(0)
    steps = pl.num_programs(0)
    local = c0.shape[0]
    up = dot_nn(low[...], wu[...]) + ub[...]
    cdf = 0.5 * (1.0 + lax.erf(up * (2.0 ** -0.5)))
    bell = jnp.exp2(up * up * (-0.5 * LOG2E)) * ((2.0 * math.pi) ** -0.5)
    act = (up * cdf).astype(BF)
    act_o[...] = act
    slope_o[...] = (cdf + up * bell).astype(BF)
    term = dot_nn(act, wd[...])

    @pl.when(step == 0)
    def _():
        acc[...] = term

    @pl.when(step > 0)
    def _():
        acc[...] += term

    @pl.when(step == steps - 1)
    def _():
        gains = jnp.zeros((1, n1.shape[1]), F32)
        shifts = jnp.zeros((1, n1.shape[1]), F32)
        downs = jnp.zeros((1, n1.shape[1]), F32)
        for at, (cot, lo) in enumerate(((c0, l0), (c1, l1), (c2, l2), (c3, l3))):
            span = pl.ds(at * local, local)
            first = n1[span, :] * gain1[...] + shift1[...]
            val = first + (acc[span, :] + db[...])
            cen = val - jnp.mean(val, -1, keepdims=True)
            r = lax.rsqrt(jnp.mean(cen * cen, -1, keepdims=True) + EPS)
            n = cen * r
            lo[...] = (n * gain2[...] + shift2[...]).astype(BF)
            dy = cot[...].astype(F32)
            dn = dy * gain2[...]
            ds = r * (dn - jnp.mean(dn, -1, keepdims=True) - n * jnp.mean(dn * n, -1, keepdims=True))
            dsec_o[span, :] = ds
            dlow = ds.astype(BF)
            dffn_o[span, :] = dlow
            gains += jnp.sum(dy * n, 0, keepdims=True)
            shifts += jnp.sum(dy, 0, keepdims=True)
            downs += jnp.sum(dlow.astype(F32), 0, keepdims=True)
        stat_o[0:1, :] = gains
        stat_o[1:2, :] = shifts
        stat_o[2:3, :] = downs
        stat_o[3:8, :] = jnp.zeros((5, stat_o.shape[1]), F32)


def ffn_fwd(low, n1, gain1, shift1, wu, ub, wd, db, gain2, shift2, cots):
    rows, width = low.shape
    inner = wu.shape[1]
    tile = 512
    steps = inner // tile
    local = cots[0].shape[0]
    one = full((1, width))
    wide = full((rows, width))
    quarter = full((local, width))
    col = pl.BlockSpec((rows, tile), lambda i: (0, i))
    grid = pl.GridSpec(
        grid=(steps,),
        in_specs=[wide, wide, one, one, pl.BlockSpec((width, tile), lambda i: (0, i)),
                  pl.BlockSpec((1, tile), lambda i: (0, i)),
                  pl.BlockSpec((tile, width), lambda i: (i, 0)), one, one, one] + [quarter] * 4,
        out_specs=[col, col] + [quarter] * 4 + [wide, wide, full((8, width))],
        scratch_shapes=[pltpu.VMEM((rows, width), F32)],
    )
    return pl.pallas_call(
        ffn_fwd_body,
        grid_spec=grid,
        out_shape=[shape_of((rows, inner), BF)] * 2 + [shape_of((local, width), BF)] * 4
        + [shape_of((rows, width), F32), shape_of((rows, width), BF), shape_of((8, width), F32)],
        compiler_params=params(),
        cost_estimate=cost(4 * rows * width * inner, 4 * width * inner + 4 * rows * inner, 2 * rows * inner),
        name="ffn_fwd",
    )(low, n1, gain1, shift1, wu, ub, wd, db, gain2, shift2, *cots)


def ffn_bwd_body(dffn, wd, slope, wu, dsec, n1, r1, gain1, wo,
                 dup_o, ubg_o, dres_o, dattn_o, dctx_o, stat_o, acc):
    step = pl.program_id(0)
    steps = pl.num_programs(0)
    dact = dot_nt(dffn[...], wd[...])
    dup = (dact * slope[...].astype(F32)).astype(BF)
    dup_o[...] = dup
    ubg_o[...] = jnp.sum(dup.astype(F32), 0, keepdims=True)
    term = dot_nt(dup, wu[...])

    @pl.when(step == 0)
    def _():
        acc[...] = term

    @pl.when(step > 0)
    def _():
        acc[...] += term

    @pl.when(step == steps - 1)
    def _():
        rows, width = n1.shape
        local = 128
        gains = jnp.zeros((1, width), F32)
        shifts = jnp.zeros((1, width), F32)
        outs = jnp.zeros((1, width), F32)
        for at in range(rows // local):
            span = pl.ds(at * local, local)
            dfirst = dsec[span, :] + acc[span, :]
            n = n1[span, :]
            dn = dfirst * gain1[...]
            r = r1[span, 0:1]
            dres = r * (dn - jnp.mean(dn, -1, keepdims=True) - n * jnp.mean(dn * n, -1, keepdims=True))
            dres_o[span, :] = dres
            dlow = dres.astype(BF)
            dattn_o[span, :] = dlow
            gains += jnp.sum(dfirst * n, 0, keepdims=True)
            shifts += jnp.sum(dfirst, 0, keepdims=True)
            outs += jnp.sum(dlow.astype(F32), 0, keepdims=True)
        stat_o[0:1, :] = gains
        stat_o[1:2, :] = shifts
        stat_o[2:3, :] = outs
        stat_o[3:8, :] = jnp.zeros((5, width), F32)
        dctx_o[...] = dot_nt(dattn_o[...], wo[...]).astype(BF)


def ffn_bwd(dffn, wd, slope, wu, dsec, n1, r1, gain1, wo):
    rows, width = dffn.shape
    inner = wu.shape[1]
    tile = 512
    steps = inner // tile
    wide = full((rows, width))
    col = pl.BlockSpec((rows, tile), lambda i: (0, i))
    grid = pl.GridSpec(
        grid=(steps,),
        in_specs=[wide, pl.BlockSpec((tile, width), lambda i: (i, 0)), col,
                  pl.BlockSpec((width, tile), lambda i: (0, i)), wide, wide, full((rows, 128)),
                  full((1, width)), full((width, width))],
        out_specs=[col, pl.BlockSpec((1, tile), lambda i: (0, i)), wide, wide, wide, full((8, width))],
        scratch_shapes=[pltpu.VMEM((rows, width), F32)],
    )
    return pl.pallas_call(
        ffn_bwd_body,
        grid_spec=grid,
        out_shape=[shape_of((rows, inner), BF), shape_of((1, inner), F32), shape_of((rows, width), F32),
                   shape_of((rows, width), BF), shape_of((rows, width), BF), shape_of((8, width), F32)],
        compiler_params=params(),
        cost_estimate=cost(4 * rows * width * inner, 4 * width * inner + 4 * rows * inner),
        name="ffn_bwd",
    )(dffn, wd, slope, wu, dsec, n1, r1, gain1, wo)


def attn_bwd_body(sc, q_r, k_r, v_r, g_r, lse, wq, wk, wv, dres,
                  dq_o, dk_o, dv_o, qbg_o, vbg_o, i0, i1, i2, i3, acc):
    step = pl.program_id(0)
    steps = pl.num_programs(0)
    rows, wide = q_r.shape
    head = wide // 2
    local = i0.shape[0]
    scale = head ** (-0.5)
    q = q_r[...]
    g = g_r[...]
    k = k_r[...]
    v = v_r[...]
    lane = lax.broadcasted_iota(jnp.int32, (rows, wide), 1)
    chunk = 256
    nchunk = rows // chunk
    dks = [[None, None] for _ in range(nchunk)]
    dvs = [[None, None] for _ in range(nchunk)]
    dqs = []
    for h in range(2):
        mine = (lane >= h * head) & (lane < (h + 1) * head)
        qh = jnp.where(mine, q, jnp.zeros_like(q))
        gh = jnp.where(mine, g, jnp.zeros_like(g))
        row = lse[pl.ds(2 * step + h, 1), :]
        ps = []
        dps = []
        delta = jnp.zeros((1, rows), F32)
        for c in range(nchunk):
            kc = k[c * chunk:(c + 1) * chunk, :]
            vc = v[c * chunk:(c + 1) * chunk, :]
            key = lax.broadcasted_iota(jnp.int32, (chunk, 1), 0) + c * chunk
            place = ((key // local) ^ sc[S_SEQ]) * local + key % local
            mask = jnp.where(place < sc[S_LEN], 0.0, -1e30).astype(F32)
            s = dot_nt(kc, qh) * (scale * LOG2E) + mask
            p = jnp.exp2(s - row)
            dp = dot_nt(vc, gh)
            delta += jnp.sum(p * dp, 0, keepdims=True)
            dvs[c][h] = dot_nn(p.astype(BF), g)
            ps.append(p)
            dps.append(dp)
        dq = None
        for c in range(nchunk):
            ds = (ps[c] * (dps[c] - delta)).astype(BF)
            dks[c][h] = dot_nn(ds, q)
            term = dot_tn(ds, k[c * chunk:(c + 1) * chunk, :])
            dq = term if dq is None else dq + term
        dqs.append(dq)
    low = lane < head
    low_c = low[:chunk, :]
    dq_o[...] = (jnp.where(low, dqs[0], dqs[1]) * scale).astype(BF)
    for c in range(nchunk):
        span = pl.ds(c * chunk, chunk)
        dk_o[span, :] = (jnp.where(low_c, dks[c][0], dks[c][1]) * scale).astype(BF)
        dv_o[span, :] = jnp.where(low_c, dvs[c][0], dvs[c][1]).astype(BF)
    dqv = dq_o[...]
    dkv = dk_o[...]
    dvv = dv_o[...]
    qbg_o[...] = jnp.sum(dqv.astype(F32), 0, keepdims=True)
    vbg_o[...] = jnp.sum(dvv.astype(F32), 0, keepdims=True)
    three = jnp.concatenate([dqv, dkv, dvv], axis=1)
    w = jnp.concatenate([wq[...], wk[...], wv[...]], axis=1)
    term = dot_nt(three, w)

    @pl.when(step == 0)
    def _():
        acc[...] = dres[...] + term

    @pl.when(step > 0)
    def _():
        acc[...] += term

    @pl.when(step == steps - 1)
    def _():
        for at, ref in enumerate((i0, i1, i2, i3)):
            ref[...] = acc[pl.ds(at * local, local), :].astype(BF)


def attn_bwd(sc, q, k, v, g, lse, qkv_w, dres, local):
    rows, width = q.shape
    pairs = HEADS // 2
    wide = width // pairs
    col = pl.BlockSpec((rows, wide), lambda i, s: (0, i))
    one = pl.BlockSpec((1, wide), lambda i, s: (0, i))
    quarter = full((local, width))
    grid = pltpu.PrefetchScalarGridSpec(
        num_scalar_prefetch=1,
        grid=(pairs,),
        in_specs=[col, col, col, col, full(lse.shape),
                  pl.BlockSpec((width, wide), lambda i, s: (0, i)),
                  pl.BlockSpec((width, wide), lambda i, s: (0, pairs + i)),
                  pl.BlockSpec((width, wide), lambda i, s: (0, 2 * pairs + i)),
                  full((rows, width))],
        out_specs=[col, col, col, one, one] + [quarter] * 4,
        scratch_shapes=[pltpu.VMEM((rows, width), F32)],
    )
    wide_bf = shape_of((rows, width), BF)
    vec = shape_of((1, width), F32)
    return pl.pallas_call(
        attn_bwd_body,
        grid_spec=grid,
        out_shape=[wide_bf, wide_bf, wide_bf, vec, vec] + [shape_of((local, width), BF)] * 4,
        compiler_params=params(),
        cost_estimate=cost(6 * rows * width * width + 10 * rows * rows * width, 12 * rows * width + 6 * width * width,
                           HEADS * rows * rows),
        name="attn_bwd",
    )(sc, q, k, v, g, lse, qkv_w, qkv_w, qkv_w, dres)


def wgrad_body(sc, la, lp, ra, rp, sa, sb, ka, kb):
    step = pl.program_id(0)
    val = (dot_tn(la[...], ra[...]) + dot_tn(lp[...], rp[...])).astype(BF)
    for at, ref in enumerate((sa, sb, ka, kb)):
        @pl.when(step == at)
        def _():
            ref[...] = val


def half_of(j, sc):
    bit = jnp.where(j % 2 == 0, sc[S_X], sc[S_Y])
    return jnp.where(j < 2, 1 - bit, bit)


def wgrad(sc, la, lp, ra, rp, maps, name):
    rows = la.shape[0]
    unit = 768
    half = unit // 2
    m_la, m_lp, m_ra, m_rp = maps
    grid = pltpu.PrefetchScalarGridSpec(
        num_scalar_prefetch=1,
        grid=(4,),
        in_specs=[pl.BlockSpec((rows, half), m_la), pl.BlockSpec((rows, half), m_lp),
                  pl.BlockSpec((rows, unit), m_ra), pl.BlockSpec((rows, unit), m_rp)],
        out_specs=[full((half, unit))] * 4,
    )
    return pl.pallas_call(
        wgrad_body,
        grid_spec=grid,
        out_shape=[shape_of((half, unit), BF)] * 4,
        compiler_params=params(),
        cost_estimate=cost(2 * 4 * half * unit * rows * 2, 8 * half * unit + 8 * rows * unit),
        name=name,
    )(sc, la, lp, ra, rp)


def wgrad_mix_body(sc, hid, hidp, ctx, ctxp, dq, dk, dv, da, r1p, r2p, sa, sb, ka, kb):
    step = pl.program_id(0)
    core = sc[S_CORE]
    first = step % 2 == 0
    for at, ref in enumerate((sa, sb, ka, kb)):
        if at % 2 == 0:
            @pl.when((step == at) & (core == 0))
            def _():
                ref[...] = (dot_tn(hid[...], dq[...]) + dot_tn(hidp[...], r1p[...])).astype(BF)

            @pl.when((step == at) & (core == 1))
            def _():
                ref[...] = (dot_tn(hid[...], dv[...]) + dot_tn(hidp[...], r1p[...])).astype(BF)
        else:
            @pl.when((step == at) & (core == 0))
            def _():
                ref[...] = (dot_tn(hid[...], dk[...]) + dot_tn(hidp[...], r2p[...])).astype(BF)

            @pl.when((step == at) & (core == 1))
            def _():
                ref[...] = (dot_tn(ctx[...], da[...]) + dot_tn(ctxp[...], r2p[...])).astype(BF)


def wgrad_mix(sc, hid, hidp, ctx, ctxp, dq, dk, dv, da, r1p, r2p):
    rows, unit = hid.shape
    half = unit // 2
    cut = pl.BlockSpec((rows, half), lambda j, s: (0, half_of(j, s)))
    wide = full((rows, unit))
    grid = pltpu.PrefetchScalarGridSpec(
        num_scalar_prefetch=1,
        grid=(4,),
        in_specs=[cut] * 4 + [wide] * 6,
        out_specs=[full((half, unit))] * 4,
    )
    return pl.pallas_call(
        wgrad_mix_body,
        grid_spec=grid,
        out_shape=[shape_of((half, unit), BF)] * 4,
        compiler_params=params(),
        cost_estimate=cost(2 * 4 * half * unit * rows * 2, 8 * half * unit + 20 * rows * unit),
        name="wgrad_mix",
    )(sc, hid, hidp, ctx, ctxp, dq, dk, dv, da, r1p, r2p)


def swap(value, axis, mask, size):
    return lax.ppermute(value, axis, [(i, i ^ mask) for i in range(size)])


def add_low(one, two):
    return (one.astype(F32) + two.astype(F32)).astype(BF)


def cut_half(value, bit, dim, keep):
    size = value.shape[dim] // 2
    at = bit if keep else 1 - bit
    return lax.dynamic_slice_in_dim(value, at * size, size, dim)


def join(own, other, bit, dim):
    return jnp.where(
        bit == 0, jnp.concatenate([own, other], dim), jnp.concatenate([other, own], dim)
    )


class Ring:
    def __init__(self, nseq, ndp, seq, dp):
        self.nseq, self.ndp, self.seq, self.dp = nseq, ndp, seq, dp
        self.x = seq & 1
        self.y = (seq >> 1) & 1
        self.dp_masks = []
        mask = 2
        while mask < ndp:
            self.dp_masks.append(mask)
            mask *= 2

    def over_x(self, value):
        return swap(value, "seq", 1, self.nseq)

    def over_y(self, value):
        return swap(value, "seq", 2, self.nseq)

    def over_dp(self, value, mask):
        return swap(value, "dp", mask, self.ndp)

    def reduce(self, sa, sb, ka, kb):
        ra = self.over_x(sa)
        rb = self.over_y(sb)
        ta = add_low(cut_half(ka, self.y, 0, False), cut_half(ra, self.y, 0, False))
        tb = add_low(cut_half(kb, self.x, 0, False), cut_half(rb, self.x, 0, False))
        ua = add_low(cut_half(ka, self.y, 0, True), cut_half(ra, self.y, 0, True))
        ub = add_low(cut_half(kb, self.x, 0, True), cut_half(rb, self.x, 0, True))
        va = self.over_y(ta)
        vb = self.over_x(tb)
        cur = jnp.stack([add_low(ua, va), add_low(ub, vb)])
        self.halved = []
        for mask in self.dp_masks:
            bit = jnp.where((self.dp & mask) != 0, 1, 0)
            if cur.shape[1] % 32 == 0:
                got = self.over_dp(cut_half(cur, bit, 1, False), mask)
                cur = add_low(cut_half(cur, bit, 1, True), got)
                self.halved.append((mask, bit))
            else:
                cur = add_low(cur, self.over_dp(cur, mask))
        return cur

    def gather(self, cur):
        for mask, bit in reversed(self.halved):
            cur = join(cur, self.over_dp(cur, mask), bit, 1)
        a, b = cur[0], cur[1]
        a = join(a, self.over_y(a), self.y, 0)
        b = join(b, self.over_x(b), self.x, 0)
        a = join(a, self.over_x(a), self.x, 0)
        b = join(b, self.over_y(b), self.y, 0)
        return a, b


def body(
    hidden_in,
    lengths,
    qkv_weight,
    query_bias,
    value_bias,
    out_weight,
    out_bias,
    attn_gain,
    attn_shift,
    up_weight,
    up_bias,
    down_weight,
    down_bias,
    ffn_gain,
    ffn_shift,
    cotangent,
):
    count, local, width = hidden_in.shape
    inner = up_weight.shape[1]
    nseq = lax.axis_size("seq")
    ndp = lax.axis_size("dp")
    seq = lax.axis_index("seq")
    dp = lax.axis_index("dp")
    core = dp & 1
    ring = Ring(nseq, ndp, seq, dp)
    line = lambda vec: vec.reshape(1, -1)

    holder = jnp.minimum(seq, count - 1)
    own_len = lax.dynamic_index_in_dim(lengths, holder, 0, False)
    own_len = jnp.where(seq < count, own_len, nseq * local)
    sc = jnp.stack([seq, own_len, core, ring.x, ring.y, core, core, core]).astype(jnp.int32)

    def to_holder(value):
        blocks = [lax.dynamic_index_in_dim(value, holder, 0, False)]
        for k in range(1, nseq):
            at = jnp.minimum(seq ^ k, count - 1)
            part = lax.dynamic_index_in_dim(value, at, 0, False)
            pairs = [(i, i ^ k) for i in range(nseq) if (i ^ k) < count]
            blocks.append(lax.ppermute(part, "seq", pairs))
        return blocks

    def from_holder(blocks):
        got = [blocks[0]]
        for k in range(1, nseq):
            pairs = [(i, i ^ k) for i in range(nseq) if i < count]
            got.append(lax.ppermute(blocks[k], "seq", pairs))
        outs = []
        for p in range(count):
            value = got[0]
            for k in range(1, nseq):
                value = jnp.where((seq ^ p) == k, got[k], value)
            outs.append(value)
        return jnp.stack(outs)

    hids = to_holder(hidden_in)
    hids, cot_in = lax.optimization_barrier((hids, cotangent))
    cots = to_holder(cot_in)
    cots[0] = jnp.where(seq < count, cots[0], jnp.zeros_like(cots[0]))

    hid, q, k, v, ctx, lse, n1, r1, low = attn_fwd(
        sc, hids, qkv_weight, line(query_bias), line(value_bias), out_weight, line(out_bias),
        line(attn_gain), line(attn_shift))
    act, slope, l0, l1, l2, l3, dsec, dffn, stat2 = ffn_fwd(
        low, n1, line(attn_gain), line(attn_shift), up_weight, line(up_bias), down_weight,
        line(down_bias), line(ffn_gain), line(ffn_shift), cots)

    def core_swap(value):
        return swap(value, "dp", 1, ndp)

    def other_cols(value):
        size = value.shape[1] // 2
        return lax.dynamic_slice_in_dim(value, (1 - core) * size, size, 1)

    act_p = core_swap(other_cols(act))
    dffn_p = core_swap(dffn)
    layer_out = from_holder([l0, l1, l2, l3])
    dup, ubg, dres, dattn, dctx, stat1 = ffn_bwd(
        dffn, down_weight, slope, up_weight, dsec, n1, r1, line(attn_gain), out_weight)
    down_parts = wgrad(
        sc, act, act_p, dffn, dffn_p,
        (lambda j, s: (0, s[S_CORE] * 4 + (j % 2) * 2 + half_of(j, s)),
         lambda j, s: (0, (j % 2) * 2 + half_of(j, s)),
         lambda j, s: (0, 0), lambda j, s: (0, 0)), "wgrad_down")
    low_p = core_swap(low)
    dup_p = core_swap(other_cols(dup))
    hid_p = core_swap(hid)
    ctx_p = core_swap(ctx)
    up_parts = wgrad(
        sc, low, low_p, dup, dup_p,
        (lambda j, s: (0, half_of(j, s)), lambda j, s: (0, half_of(j, s)),
         lambda j, s: (0, s[S_CORE] * 2 + j % 2), lambda j, s: (0, j % 2)), "wgrad_up")
    dq, dk, dv, qbg, vbg, i0, i1, i2, i3 = attn_bwd(sc, q, k, v, dctx, lse, qkv_weight, dres, local)
    input_grad = from_holder([i0, i1, i2, i3])
    r1_p = core_swap(jnp.where(core == 0, dv, dq))
    r2_p = core_swap(jnp.where(core == 0, dattn, dk))
    mix_parts = wgrad_mix(sc, hid, hid_p, ctx, ctx_p, dq, dk, dv, dattn, r1_p, r2_p)

    small = jnp.concatenate(
        [stat2[0:3].reshape(-1), stat1[0:3].reshape(-1), qbg.reshape(-1), vbg.reshape(-1), ubg.reshape(-1)]
    ).reshape(-1, 128)
    mask = 1
    while mask < nseq:
        small = small + swap(small, "seq", mask, nseq)
        mask *= 2
    mask = 1
    while mask < ndp:
        small = small + swap(small, "dp", mask, ndp)
        mask *= 2
    small = small.reshape(-1)
    vec = [small[i * width:(i + 1) * width] for i in range(8)]
    up_bias_grad = small[8 * width:]

    def finish(parts):
        a, b = ring.gather(ring.reduce(*parts))
        pa = core_swap(a)
        pb = core_swap(b)
        return a, b, pa, pb

    def ordered(parts):
        a, b, pa, pb = parts
        lo = core == 0
        return (jnp.where(lo, a, pa), jnp.where(lo, b, pb), jnp.where(lo, pa, a), jnp.where(lo, pb, b))

    d_parts = ordered(finish(down_parts))
    u_parts = ordered(finish(up_parts))
    m_parts = ordered(finish(mix_parts))
    down_grad = jnp.concatenate(d_parts, 0).astype(F32)
    up_grad = jnp.concatenate(u_parts, 1).astype(F32)
    qkv_grad = jnp.concatenate(m_parts[:3], 1).astype(F32)
    out_grad = m_parts[3].astype(F32)
    return (
        layer_out,
        input_grad,
        qkv_grad,
        vec[6],
        vec[7],
        out_grad,
        vec[5],
        vec[3],
        vec[4],
        up_grad,
        up_bias_grad,
        down_grad,
        vec[2],
        vec[0],
        vec[1],
    )


def solution(mesh):
    split = P("dp", "seq", None)
    return jax.shard_map(
        body,
        mesh=mesh,
        in_specs=(split, P("dp")) + (P(),) * 13 + (split,),
        out_specs=(split, split) + (P(),) * 13,
        check_vma=False,
    )
```

```python
import functools
import math

import jax
import jax.numpy as jnp
from jax import lax
from jax.experimental import pallas as pl
from jax.experimental.pallas import tpu as pltpu
from jax.sharding import PartitionSpec as P

HEADS = 12
EPS = 1e-12
BF = jnp.bfloat16
F32 = jnp.float32
VMEM_LIMIT = 60 * 1024 * 1024
LOG2E = math.log2(math.e)
HALVINGS = 4
S_SEQ, S_LEN, S_CORE = range(3)
S_FIRST = 3
S_FIRST_MIX = S_FIRST + HALVINGS


def dot_nn(left, right):
    return lax.dot_general(left, right, (((1,), (0,)), ((), ())), preferred_element_type=F32)


def dot_nt(left, right):
    return lax.dot_general(left, right, (((1,), (1,)), ((), ())), preferred_element_type=F32)


def dot_tn(left, right):
    return lax.dot_general(left, right, (((0,), (0,)), ((), ())), preferred_element_type=F32)


def params(flag=None):
    return pltpu.CompilerParams(vmem_limit_bytes=VMEM_LIMIT)


def cost(flops, nbytes, trans=0):
    return pl.CostEstimate(flops=int(flops), bytes_accessed=int(nbytes), transcendentals=int(trans))


def full(shape):
    zeros = (0,) * len(shape)
    return pl.BlockSpec(shape, lambda *_: zeros)


def shape_of(shape, dtype):
    return jax.ShapeDtypeStruct(shape, dtype)


def attn_fwd_body(sc, h0, h1, h2, h3, wq, wk, wv, qb, vb, wo, ob, gain, shift,
                  hlc, q_o, k_o, v_o, lse_o, n1_o, r1_o, acc, lse_s):
    step = pl.program_id(0)
    steps = pl.num_programs(0)
    local, width = h0.shape
    rows = hlc.shape[0]
    head = wq.shape[1] // 2
    wide = 2 * head

    @pl.when(step == 0)
    def _():
        for at, ref in enumerate((h0, h1, h2, h3)):
            hlc[at * local:(at + 1) * local, width:2 * width] = ref[...]
        acc[...] = jnp.zeros_like(acc)
        lse_s[...] = jnp.zeros_like(lse_s)

    x = hlc[:, width:2 * width]
    w = jnp.concatenate([wq[...], wk[...], wv[...]], axis=1)
    both = dot_nn(x, w)
    q_o[...] = (both[:, :wide] + qb[...]).astype(BF)
    k_o[...] = both[:, wide:2 * wide].astype(BF)
    v_o[...] = (both[:, 2 * wide:] + vb[...]).astype(BF)
    k = k_o[...]
    v = v_o[...]
    key = lax.broadcasted_iota(jnp.int32, (1, rows), 1)
    place = ((key // local) ^ sc[S_SEQ]) * local + key % local
    mask = jnp.where(place < sc[S_LEN], 0.0, -1e30).astype(F32)
    scale = head ** (-0.5) * LOG2E
    chunk = rows
    lane = lax.broadcasted_iota(jnp.int32, (chunk, wide), 1)
    lane_l = lax.broadcasted_iota(jnp.int32, (chunk, lse_s.shape[1]), 1)
    for part in range(rows // chunk):
        span = pl.ds(part * chunk, chunk)
        q = q_o[span, :]
        outs = []
        tops = []
        for h in range(2):
            mine = (lane >= h * head) & (lane < (h + 1) * head)
            qh = jnp.where(mine, q, jnp.zeros_like(q))
            s = dot_nt(qh, k) * scale + mask
            top = jnp.max(s, -1, keepdims=True)
            e = jnp.exp2(s - top)
            total = jnp.sum(e, -1, keepdims=True)
            pv = dot_nn(e.astype(BF), v)
            outs.append(pv / total)
            tops.append(top + jnp.log2(total))
        ctx = jnp.where(lane < head, outs[0], outs[1]).astype(BF)
        hlc[span, pl.ds(pl.multiple_of(2 * width + step * wide, wide), wide)] = ctx
        acc[span, :] += dot_nn(ctx, wo[...])
        old = lse_s[span, :]
        old = jnp.where(lane_l == 2 * step, tops[0], old)
        lse_s[span, :] = jnp.where(lane_l == 2 * step + 1, tops[1], old)

    @pl.when(step == steps - 1)
    def _():
        lse_o[...] = jnp.transpose(lse_s[...])[:lse_o.shape[0], :]

        @pl.loop(0, rows // local)
        def _(part):
            span = pl.ds(pl.multiple_of(part * local, local), local)
            val = hlc[span, width:2 * width].astype(F32) + (acc[span, :] + ob[...])
            cen = val - jnp.mean(val, -1, keepdims=True)
            r = lax.rsqrt(jnp.mean(cen * cen, -1, keepdims=True) + EPS)
            n = cen * r
            n1_o[span, :] = n
            r1_o[span, :] = jnp.broadcast_to(r, (local, r1_o.shape[1]))
            hlc[span, :width] = (n * gain[...] + shift[...]).astype(BF)


def attn_fwd(sc, blocks, qkv_w, qb, vb, out_w, ob, gain, shift):
    local, width = blocks[0].shape
    rows = local * len(blocks)
    pairs = HEADS // 2
    wide = width // pairs
    row = lambda i, s: (0, i)
    grid = pltpu.PrefetchScalarGridSpec(
        num_scalar_prefetch=1,
        grid=(pairs,),
        in_specs=[full((local, width))] * 4 + [
            pl.BlockSpec((width, wide), lambda i, s: (0, i)),
            pl.BlockSpec((width, wide), lambda i, s: (0, pairs + i)),
            pl.BlockSpec((width, wide), lambda i, s: (0, 2 * pairs + i)),
            pl.BlockSpec((1, wide), row),
            pl.BlockSpec((1, wide), row),
            pl.BlockSpec((wide, width), lambda i, s: (i, 0)),
            full((1, width)), full((1, width)), full((1, width)),
        ],
        out_specs=[
            full((rows, 3 * width)),
            pl.BlockSpec((rows, wide), row),
            pl.BlockSpec((rows, wide), row),
            pl.BlockSpec((rows, wide), row),
            full((16, rows)),
            full((rows, width)),
            full((rows, 128)),
        ],
        scratch_shapes=[pltpu.VMEM((rows, width), F32), pltpu.VMEM((rows, 128), F32)],
    )
    wide_bf = shape_of((rows, width), BF)
    return pl.pallas_call(
        attn_fwd_body,
        grid_spec=grid,
        out_shape=[shape_of((rows, 3 * width), BF), wide_bf, wide_bf, wide_bf, shape_of((16, rows), F32),
                   shape_of((rows, width), F32), shape_of((rows, 128), F32)],
        compiler_params=params(),
        cost_estimate=cost(2 * rows * width * width * 4 + 4 * rows * rows * width, 12 * rows * width + 8 * width * width,
                           HEADS * rows * rows),
        name="attn_fwd",
    )(sc, *blocks, qkv_w, qkv_w, qkv_w, qb, vb, out_w, ob, gain, shift)


def ffn_fwd_body(sc, low, n1, gain1, shift1, wu, ub, wd, db, gain2, shift2, c0, c1, c2, c3,
                 act_o, slope_o, send_o, lo_o, dsec_o, stat_o, acc):
    step = pl.program_id(0)
    steps = pl.num_programs(0)
    local, width = c0.shape
    tile = wu.shape[1]
    up = dot_nn(low[...], wu[...]) + ub[...]
    cdf = 0.5 * (1.0 + lax.erf(up * (2.0 ** -0.5)))
    bell = jnp.exp2(up * up * (-0.5 * LOG2E)) * ((2.0 * math.pi) ** -0.5)
    act = (up * cdf).astype(BF)
    act_o[...] = act
    slope_o[...] = (cdf + up * bell).astype(BF)
    base = (1 - sc[S_CORE]) * (steps // 2)

    @pl.when((step >= base) & (step < base + steps // 2))
    def _():
        send_o[:, pl.ds(pl.multiple_of((step - base) * tile, tile), tile)] = act_o[...]

    term = dot_nn(act, wd[...])

    @pl.when(step == 0)
    def _():
        acc[...] = term

    @pl.when(step > 0)
    def _():
        acc[...] += term

    @pl.when(step == steps - 1)
    def _():
        stat_o[...] = jnp.zeros_like(stat_o)
        for at, cot in enumerate((c0, c1, c2, c3)):
            span = pl.ds(at * local, local)
            first = n1[span, :] * gain1[...] + shift1[...]
            val = first + (acc[span, :] + db[...])
            cen = val - jnp.mean(val, -1, keepdims=True)
            r = lax.rsqrt(jnp.mean(cen * cen, -1, keepdims=True) + EPS)
            n = cen * r
            lo_o[span, :] = (n * gain2[...] + shift2[...]).astype(BF)
            dy = cot[...].astype(F32)
            dn = dy * gain2[...]
            ds = r * (dn - jnp.mean(dn, -1, keepdims=True) - n * jnp.mean(dn * n, -1, keepdims=True))
            dsec_o[span, :] = ds
            dlow = ds.astype(BF)
            send_o[span, send_o.shape[1] - width:] = dlow
            stat_o[0:1, :] += jnp.sum(dy * n, 0, keepdims=True)
            stat_o[1:2, :] += jnp.sum(dy, 0, keepdims=True)
            stat_o[2:3, :] += jnp.sum(dlow.astype(F32), 0, keepdims=True)


def ffn_fwd(sc, hlc, n1, gain1, shift1, wu, ub, wd, db, gain2, shift2, cots):
    rows, width = n1.shape
    inner = wu.shape[1]
    tile = width
    steps = inner // tile
    local = cots[0].shape[0]
    one = full((1, width))
    wide = full((rows, width))
    quarter = full((local, width))
    col = pl.BlockSpec((rows, tile), lambda i, s: (0, i))
    grid = pltpu.PrefetchScalarGridSpec(
        num_scalar_prefetch=1,
        grid=(steps,),
        in_specs=[wide, wide, one, one, pl.BlockSpec((width, tile), lambda i, s: (0, i)),
                  pl.BlockSpec((1, tile), lambda i, s: (0, i)),
                  pl.BlockSpec((tile, width), lambda i, s: (i, 0)), one, one, one] + [quarter] * 4,
        out_specs=[col, col, full((rows, inner // 2 + width)), wide, wide, full((8, width))],
        scratch_shapes=[pltpu.VMEM((rows, width), F32)],
    )
    return pl.pallas_call(
        ffn_fwd_body,
        grid_spec=grid,
        out_shape=[shape_of((rows, inner), BF)] * 2 + [shape_of((rows, inner // 2 + width), BF),
                   shape_of((rows, width), BF), shape_of((rows, width), F32), shape_of((8, width), F32)],
        compiler_params=params(),
        cost_estimate=cost(4 * rows * width * inner, 4 * width * inner + 4 * rows * inner, 2 * rows * inner),
        name="ffn_fwd",
    )(sc, hlc, n1, gain1, shift1, wu, ub, wd, db, gain2, shift2, *cots)


def ffn_bwd_body(sc, dffn, wd, slope, wu, dsec, n1, r1, gain1, wo,
                 dup_o, send_o, dres_o, dattn_o, dctx_o, stat_o, acc):
    step = pl.program_id(0)
    steps = pl.num_programs(0)
    tile = wu.shape[1]
    dact = dot_nt(dffn[...], wd[...])
    dup = (dact * slope[...].astype(F32)).astype(BF)
    dup_o[...] = dup
    stat_o[pl.ds(4 + step, 1), :] = jnp.sum(dup.astype(F32), 0, keepdims=True)
    base = (1 - sc[S_CORE]) * (steps // 2)

    @pl.when((step >= base) & (step < base + steps // 2))
    def _():
        send_o[:, pl.ds(pl.multiple_of((step - base) * tile, tile), tile)] = dup_o[...]

    term = dot_nt(dup, wu[...])

    @pl.when(step == 0)
    def _():
        acc[...] = term

    @pl.when(step > 0)
    def _():
        acc[...] += term

    @pl.when(step == steps - 1)
    def _():
        rows, width = n1.shape
        local = 128
        stat_o[0:4, :] = jnp.zeros((4, width), F32)
        for at in range(rows // local):
            span = pl.ds(at * local, local)
            dfirst = dsec[span, :] + acc[span, :]
            n = n1[span, :]
            dn = dfirst * gain1[...]
            r = r1[span, 0:1]
            dres = r * (dn - jnp.mean(dn, -1, keepdims=True) - n * jnp.mean(dn * n, -1, keepdims=True))
            dres_o[span, :] = dres
            dlow = dres.astype(BF)
            dattn_o[span, :] = dlow
            stat_o[0:1, :] += jnp.sum(dfirst * n, 0, keepdims=True)
            stat_o[1:2, :] += jnp.sum(dfirst, 0, keepdims=True)
            stat_o[2:3, :] += jnp.sum(dlow.astype(F32), 0, keepdims=True)
        dctx_o[...] = dot_nt(dattn_o[...], wo[...]).astype(BF)


def ffn_bwd(sc, send, wd, slope, wu, dsec, n1, r1, gain1, wo):
    rows, width = dsec.shape
    inner = wu.shape[1]
    tile = width
    steps = inner // tile
    wide = full((rows, width))
    last = send.shape[1] // width - 1
    col = pl.BlockSpec((rows, tile), lambda i, s: (0, i))
    grid = pltpu.PrefetchScalarGridSpec(
        num_scalar_prefetch=1,
        grid=(steps,),
        in_specs=[pl.BlockSpec((rows, width), lambda i, s: (0, last)),
                  pl.BlockSpec((tile, width), lambda i, s: (i, 0)), col,
                  pl.BlockSpec((width, tile), lambda i, s: (0, i)), wide, wide, full((rows, 128)),
                  full((1, width)), full((width, width))],
        out_specs=[col, full((rows, inner // 2)), wide, wide, wide, full((8, width))],
        scratch_shapes=[pltpu.VMEM((rows, width), F32)],
    )
    return pl.pallas_call(
        ffn_bwd_body,
        grid_spec=grid,
        out_shape=[shape_of((rows, inner), BF), shape_of((rows, inner // 2), BF), shape_of((rows, width), F32),
                   shape_of((rows, width), BF), shape_of((rows, width), BF), shape_of((8, width), F32)],
        compiler_params=params(),
        cost_estimate=cost(4 * rows * width * inner, 4 * width * inner + 4 * rows * inner),
        name="ffn_bwd",
    )(sc, send, wd, slope, wu, dsec, n1, r1, gain1, wo)


def split_terms(value):
    high = value.astype(BF)
    return high, (value - high.astype(F32)).astype(BF)


def attn_bwd_body(sc, q_r, k_r, v_r, g_r, lse, wq, wk, wv, dres, da_r, lo, stat1, stat2,
                  dq_o, dk_o, dv_o, send_o, small_o, i0, i1, i2, i3, acc):
    step = pl.program_id(0)
    steps = pl.num_programs(0)
    rows, wide = q_r.shape
    head = wide // 2
    local = i0.shape[0] // 2
    scale = head ** (-0.5)
    q = q_r[...]
    g = g_r[...]
    k = k_r[...]
    v = v_r[...]
    lane = lax.broadcasted_iota(jnp.int32, (rows, wide), 1)
    chunk = rows
    nchunk = rows // chunk
    dks = [[None, None] for _ in range(nchunk)]
    dvs = [[None, None] for _ in range(nchunk)]
    dqs = []
    for h in range(2):
        mine = (lane >= h * head) & (lane < (h + 1) * head)
        qh = jnp.where(mine, q, jnp.zeros_like(q))
        gh = jnp.where(mine, g, jnp.zeros_like(g))
        row = lse[pl.ds(2 * step + h, 1), :]
        ps = []
        dps = []
        delta = jnp.zeros((1, rows), F32)
        for c in range(nchunk):
            kc = k[c * chunk:(c + 1) * chunk, :]
            vc = v[c * chunk:(c + 1) * chunk, :]
            key = lax.broadcasted_iota(jnp.int32, (chunk, 1), 0) + c * chunk
            place = ((key // local) ^ sc[S_SEQ]) * local + key % local
            mask = jnp.where(place < sc[S_LEN], 0.0, -1e30).astype(F32)
            s = dot_nt(kc, qh) * (scale * LOG2E) + mask
            p = jnp.exp2(s - row)
            dp = dot_nt(vc, gh)
            delta += jnp.sum(p * dp, 0, keepdims=True)
            dvs[c][h] = dot_nn(p.astype(BF), g)
            ps.append(p)
            dps.append(dp)
        dq = None
        for c in range(nchunk):
            ds = (ps[c] * (dps[c] - delta)).astype(BF)
            dks[c][h] = dot_nn(ds, q)
            term = dot_tn(ds, k[c * chunk:(c + 1) * chunk, :])
            dq = term if dq is None else dq + term
        dqs.append(dq)
    low = lane < head
    low_c = low[:chunk, :]
    dq_o[...] = (jnp.where(low, dqs[0], dqs[1]) * scale).astype(BF)
    for c in range(nchunk):
        span = pl.ds(c * chunk, chunk)
        dk_o[span, :] = (jnp.where(low_c, dks[c][0], dks[c][1]) * scale).astype(BF)
        dv_o[span, :] = jnp.where(low_c, dvs[c][0], dvs[c][1]).astype(BF)
    dqv = dq_o[...]
    dkv = dk_o[...]
    dvv = dv_o[...]
    here = pl.ds(pl.multiple_of(step * wide, wide), wide)
    small_o[6:7, here] = jnp.sum(dqv.astype(F32), 0, keepdims=True)
    small_o[7:8, here] = jnp.sum(dvv.astype(F32), 0, keepdims=True)

    @pl.when(sc[S_CORE] == 0)
    def _():
        send_o[0:rows, here] = dv_o[...]
        send_o[rows:2 * rows, here] = da_r[...]

    @pl.when(sc[S_CORE] != 0)
    def _():
        send_o[0:rows, here] = dq_o[...]
        send_o[rows:2 * rows, here] = dk_o[...]

    three = jnp.concatenate([dqv, dkv, dvv], axis=1)
    w = jnp.concatenate([wq[...], wk[...], wv[...]], axis=1)
    term = dot_nt(three, w)

    @pl.when(step == 0)
    def _():
        acc[...] = dres[...] + term

    @pl.when(step > 0)
    def _():
        acc[...] += term

    @pl.when(step == steps - 1)
    def _():
        for at, ref in enumerate((i0, i1, i2, i3)):
            ref[0:local, :] = lo[at * local:(at + 1) * local, :]
            ref[local:2 * local, :] = acc[pl.ds(at * local, local), :].astype(BF)
        small_o[0:3, :] = stat2[0:3, :]
        small_o[3:6, :] = stat1[0:3, :]
        small_o[8:12, :] = stat1[4:8, :]
        small_o[12:16, :] = jnp.zeros((4, small_o.shape[1]), F32)
        high, rest = split_terms(small_o[...])
        send_o[2 * rows:2 * rows + 16, :] = high
        send_o[2 * rows + 16:2 * rows + 32, :] = rest


def attn_bwd(sc, q, k, v, g, lse, qkv_w, dres, dattn, lo, stat1, stat2, local):
    rows, width = q.shape
    pairs = HEADS // 2
    wide = width // pairs
    col = pl.BlockSpec((rows, wide), lambda i, s: (0, i))
    quarter = full((2 * local, width))
    grid = pltpu.PrefetchScalarGridSpec(
        num_scalar_prefetch=1,
        grid=(pairs,),
        in_specs=[col, col, col, col, full(lse.shape),
                  pl.BlockSpec((width, wide), lambda i, s: (0, i)),
                  pl.BlockSpec((width, wide), lambda i, s: (0, pairs + i)),
                  pl.BlockSpec((width, wide), lambda i, s: (0, 2 * pairs + i)),
                  full((rows, width)), col, full((rows, width)), full((8, width)), full((8, width))],
        out_specs=[col, col, col, full((2 * rows + 32, width)), full((16, width))] + [quarter] * 4,
        scratch_shapes=[pltpu.VMEM((rows, width), F32)],
    )
    wide_bf = shape_of((rows, width), BF)
    return pl.pallas_call(
        attn_bwd_body,
        grid_spec=grid,
        out_shape=[wide_bf, wide_bf, wide_bf, shape_of((2 * rows + 32, width), BF),
                   shape_of((16, width), F32)] + [shape_of((2 * local, width), BF)] * 4,
        compiler_params=params(),
        cost_estimate=cost(6 * rows * width * width + 10 * rows * rows * width, 12 * rows * width + 6 * width * width,
                           HEADS * rows * rows),
        name="attn_bwd",
    )(sc, q, k, v, g, lse, qkv_w, qkv_w, qkv_w, dres, dattn, lo, stat1, stat2)


def wgrad_body(sc, la, lp, ra, rp, *refs):
    step = pl.program_id(0)
    send, keep = refs[-2:]
    val = (dot_tn(la[...], ra[...]) + dot_tn(lp[...], rp[...])).astype(BF)

    @pl.when(step < 2)
    def _():
        send[...] = val

    @pl.when(step >= 2)
    def _():
        keep[...] = val


def half_of(j, sc):
    return jnp.where(j < 2, 1 - sc[S_FIRST], sc[S_FIRST])


def wgrad(sc, la, lp, ra, rp, maps, at, units, into, name):
    rows = la.shape[0]
    unit = ra.shape[1] if ra.shape[1] < 768 else 768
    half = unit // 2
    m_la, m_lp, m_ra, m_rp = maps
    grid = pltpu.PrefetchScalarGridSpec(
        num_scalar_prefetch=1,
        grid=(4,),
        in_specs=[pl.BlockSpec((rows, half), m_la), pl.BlockSpec((rows, half), m_lp),
                  pl.BlockSpec((rows, unit), m_ra), pl.BlockSpec((rows, unit), m_rp)]
        + [pl.BlockSpec(memory_space=pl.ANY)] * len(into),
        out_specs=[pl.BlockSpec((half, unit), lambda j, s: (at + jnp.minimum(j, 1), 0)),
                   pl.BlockSpec((half, unit), lambda j, s: (at + jnp.maximum(j - 2, 0), 0))],
    )
    return pl.pallas_call(
        wgrad_body,
        grid_spec=grid,
        out_shape=[shape_of((units * half, unit), BF)] * 2,
        input_output_aliases={5 + i: i for i in range(len(into))},
        compiler_params=params(),
        cost_estimate=cost(2 * 4 * half * unit * rows * 2, 8 * half * unit + 8 * rows * unit),
        name=name,
    )(sc, la, lp, ra, rp, *into)


def wgrad_mix_body(sc, hid, hidp, ctx, ctxp, dq, dk, dv, da, peer, small, send, keep, small_o):
    step = pl.program_id(0)
    core = sc[S_CORE]
    rows, unit = dq.shape
    half = unit // 2

    def put(val):
        val = val.astype(BF)

        @pl.when(step < 2)
        def _():
            send[pl.ds(pl.multiple_of(step * half, half), half), :] = val

        @pl.when(step >= 2)
        def _():
            keep[pl.ds(pl.multiple_of((step - 2) * half, half), half), :] = val

    @pl.when(step % 2 == 0)
    def _():
        @pl.when(core == 0)
        def _():
            put(dot_tn(hid[...], dq[...]) + dot_tn(hidp[...], peer[0:rows, :]))

        @pl.when(core != 0)
        def _():
            put(dot_tn(hid[...], dv[...]) + dot_tn(hidp[...], peer[0:rows, :]))

    @pl.when(step % 2 == 1)
    def _():
        @pl.when(core == 0)
        def _():
            put(dot_tn(hid[...], dk[...]) + dot_tn(hidp[...], peer[rows:2 * rows, :]))

        @pl.when(core != 0)
        def _():
            put(dot_tn(ctx[...], da[...]) + dot_tn(ctxp[...], peer[rows:2 * rows, :]))

    @pl.when(step == 0)
    def _():
        got = peer[2 * rows:2 * rows + 16, :].astype(F32) + peer[2 * rows + 16:2 * rows + 32, :].astype(F32)
        val = small[...] + got
        small_o[...] = val
        high, rest = split_terms(val)
        send[unit:unit + 16, :] = high
        send[unit + 16:unit + 32, :] = rest


def wgrad_mix(sc, hlc, hlcp, dq, dk, dv, da, peer, small):
    rows, unit = dq.shape
    half = unit // 2

    def cut(at):
        return pl.BlockSpec((rows, half), lambda j, s: (0, at + jnp.where(j < 2, 1 - s[S_FIRST_MIX], s[S_FIRST_MIX])))

    wide = full((rows, unit))
    grid = pltpu.PrefetchScalarGridSpec(
        num_scalar_prefetch=1,
        grid=(4,),
        in_specs=[cut(2), cut(2), cut(4), cut(4)] + [wide] * 4 + [full(peer.shape), full(small.shape)],
        out_specs=[full((unit + 32, unit)), full((unit, unit)), full(small.shape)],
    )
    return pl.pallas_call(
        wgrad_mix_body,
        grid_spec=grid,
        out_shape=[shape_of((unit + 32, unit), BF), shape_of((unit, unit), BF), shape_of(small.shape, F32)],
        compiler_params=params(),
        cost_estimate=cost(2 * 4 * half * unit * rows * 2, 8 * half * unit + 20 * rows * unit),
        name="wgrad_mix",
    )(sc, hlc, hlcp, hlc, hlcp, dq, dk, dv, da, peer, small)


def fold_body(sc, keep, got, *refs, units, bit_at):
    last = bit_at is None
    small = refs[0] if len(refs) in (3, 4) and not last else None
    rows = keep.shape[0] // units
    if last:
        out = refs[-1] if len(refs) == 1 else refs[1]
        out[...] = (keep[...].astype(F32) + got[0:units * rows, :].astype(F32)).astype(BF)
        if len(refs) > 1:
            low = units * rows
            refs[2][...] = refs[0][...] + got[low:low + 16, :].astype(F32) + got[low + 16:low + 32, :].astype(F32)
        return
    half = rows // 2
    bit = sc[bit_at]
    if small is None:
        send_o, keep_o = refs
    else:
        send_o, keep_o, small_o = refs[1:]
    for u in range(units):
        go = pl.ds(pl.multiple_of(u * rows + (1 - bit) * half, 16), half)
        stay = pl.ds(pl.multiple_of(u * rows + bit * half, 16), half)
        send_o[u * half:(u + 1) * half, :] = (keep[go, :].astype(F32) + got[go, :].astype(F32)).astype(BF)
        keep_o[u * half:(u + 1) * half, :] = (keep[stay, :].astype(F32) + got[stay, :].astype(F32)).astype(BF)
    if small is not None:
        low = units * rows
        val = small[...] + (got[low:low + 16, :].astype(F32) + got[low + 16:low + 32, :].astype(F32))
        small_o[...] = val
        high, rest = split_terms(val)
        send_o[units * half:units * half + 16, :] = high
        send_o[units * half + 16:units * half + 32, :] = rest


def fold(sc, keep, got, small, units, bit_at):
    rows, width = keep.shape
    vmem = pl.BlockSpec(memory_space=pltpu.VMEM)
    extra = 0 if small is None else 32
    if bit_at is None:
        outs = [shape_of((rows, width), BF)]
    else:
        outs = [shape_of((rows // 2 + extra, width), BF), shape_of((rows // 2, width), BF)]
    args = [keep, got]
    if small is not None:
        outs.append(shape_of(small.shape, F32))
        args.append(small)
    return pl.pallas_call(
        functools.partial(fold_body, units=units, bit_at=bit_at),
        out_shape=outs,
        in_specs=[pl.BlockSpec(memory_space=pltpu.SMEM)] + [vmem] * len(args),
        out_specs=[vmem] * len(outs),
        compiler_params=params(),
        cost_estimate=cost(2 * rows * width, 6 * rows * width),
        name="fold",
    )(sc, *args)


def swap(value, axis, mask, size):
    return lax.ppermute(value, axis, [(i, i ^ mask) for i in range(size)])


def join(own, other, bit, units):
    rows = own.shape[0] // units
    own = own.reshape(units, rows, own.shape[1])
    other = other.reshape(units, rows, other.shape[1])
    both = jnp.where(
        bit == 0, jnp.concatenate([own, other], 1), jnp.concatenate([other, own], 1)
    )
    return both.reshape(2 * units * rows, own.shape[2])


class Piece:
    def __init__(self, units, masks, bits, at, members):
        self.units, self.masks, self.bits, self.at, self.members = units, masks, bits, at, members

    def permute(self, value, stage):
        pairs = [(i, i ^ self.masks[i & 1][stage]) for i in range(self.members)]
        return lax.ppermute(value, ("seq", "dp"), pairs)


def after(token, *values):
    return lax.optimization_barrier((token,) + values)[1:]


def corner(value):
    return value[:8, :128]


def body(
    hidden_in,
    lengths,
    qkv_weight,
    query_bias,
    value_bias,
    out_weight,
    out_bias,
    attn_gain,
    attn_shift,
    up_weight,
    up_bias,
    down_weight,
    down_bias,
    ffn_gain,
    ffn_shift,
    cotangent,
):
    count, local, width = hidden_in.shape
    nseq = lax.axis_size("seq")
    ndp = lax.axis_size("dp")
    seq = lax.axis_index("seq")
    dp = lax.axis_index("dp")
    core = dp & 1
    flat = seq * ndp + dp
    members = nseq * ndp
    line = lambda vec: vec.reshape(1, -1)

    x_mask, y_mask = ndp, 2 * ndp
    dp_masks = []
    mask = 2
    while mask < ndp:
        dp_masks.append(mask)
        mask *= 2
    z_mask, rest = dp_masks[0], dp_masks[1:]

    def piece(units, orders, at):
        masks = [list(order) + rest for order in orders]
        bits = []
        for stage in range(len(masks[0])):
            pick = jnp.where(core == 0, masks[0][stage], masks[1][stage])
            bits.append(jnp.where((flat & pick) != 0, 1, 0))
        return Piece(units, masks, bits, at, members)

    big = piece(4, [(x_mask, y_mask, z_mask), (y_mask, z_mask, x_mask)], S_FIRST)
    mix = piece(2, [(z_mask, x_mask, y_mask), (x_mask, z_mask, y_mask)], S_FIRST_MIX)

    holder = jnp.minimum(seq, count - 1)
    own_len = lax.dynamic_index_in_dim(lengths, holder, 0, False)
    own_len = jnp.where(seq < count, own_len, nseq * local)
    sc = jnp.stack([seq, own_len, core] + big.bits[:HALVINGS] + mix.bits[:HALVINGS]).astype(jnp.int32)

    def to_holder(value):
        blocks = [lax.dynamic_index_in_dim(value, holder, 0, False)]
        parts = [lax.dynamic_index_in_dim(value, jnp.minimum(seq ^ k, count - 1), 0, False) for k in range(1, nseq)]
        for k in range(1, nseq):
            pairs = [(i, i ^ k) for i in range(nseq) if (i ^ k) < count]
            blocks.append(lax.ppermute(parts[k - 1], "seq", pairs))
        return blocks

    hids = to_holder(hidden_in)
    cots = to_holder(cotangent)
    cots[0] = jnp.where(seq < count, cots[0], jnp.zeros_like(cots[0]))

    hlc, q, k, v, lse, n1, r1 = attn_fwd(
        sc, hids, qkv_weight, line(query_bias), line(value_bias), out_weight, line(out_bias),
        line(attn_gain), line(attn_shift))

    def core_swap(value):
        return swap(value, "dp", 1, ndp)

    hlc_p = core_swap(hlc)
    act, slope, send, lo, dsec, stat2 = ffn_fwd(
        sc, hlc, n1, line(attn_gain), line(attn_shift), up_weight, line(up_bias), down_weight,
        line(down_bias), line(ffn_gain), line(ffn_shift), cots)
    act_p = core_swap(send)
    dup, dup_send, dres, dattn, dctx, stat1 = ffn_bwd(
        sc, send, down_weight, slope, up_weight, dsec, n1, r1, line(attn_gain), out_weight)
    dup_p = core_swap(dup_send)
    last = send.shape[1] // width - 1
    into = wgrad(
        sc, act, act_p, send, act_p,
        (lambda j, s: (0, s[S_CORE] * 4 + (j % 2) * 2 + half_of(j, s)),
         lambda j, s: (0, (j % 2) * 2 + half_of(j, s)),
         lambda j, s: (0, last), lambda j, s: (0, last)), 0, 4, (), "wgrad_down")
    send1, keep1 = wgrad(
        sc, hlc, hlc_p, dup, dup_p,
        (lambda j, s: (0, half_of(j, s)), lambda j, s: (0, half_of(j, s)),
         lambda j, s: (0, s[S_CORE] * 2 + j % 2), lambda j, s: (0, j % 2)), 2, 4, into, "wgrad_up")
    got1 = big.permute(send1, 0)
    (dctx,) = after(corner(keep1), dctx)
    dq, dk, dv, peer_send, small, i0, i1, i2, i3 = attn_bwd(
        sc, q, k, v, dctx, lse, qkv_weight, dres, dattn, lo, stat1, stat2, local)
    peer = core_swap(peer_send)
    send2, keep2, small = wgrad_mix(sc, hlc, hlc_p, dq, dk, dv, dattn, peer, small)
    got2 = mix.permute(send2, 0)
    token = corner(keep2)

    big_stages = len(big.bits)
    done1, done2 = [], []
    for stage in range(big_stages):
        halve = stage + 1 < min(HALVINGS, big_stages)
        more = stage + 1 < big_stages
        keep1, got1 = after(token, keep1, got1)
        if halve:
            send1, keep1 = fold(sc, keep1, got1, None, big.units, big.at + stage + 1)
        else:
            (keep1,) = fold(sc, keep1, got1, None, big.units, None)
            send1 = keep1
        token = corner(keep1)
        if more:
            got1 = big.permute(send1, stage + 1)
        if stage == 0:
            blocks = after(token, i0, i1, i2, i3)
            back = [blocks[0]]
            for k_at in range(1, nseq):
                pairs = [(i, i ^ k_at) for i in range(nseq) if i < count]
                back.append(lax.ppermute(blocks[k_at], "seq", pairs))
        keep2, got2, small = after(token, keep2, got2, small)
        if halve:
            send2, keep2, small = fold(sc, keep2, got2, small, mix.units, mix.at + stage + 1)
        else:
            keep2, small = fold(sc, keep2, got2, small, mix.units, None)
            if more:
                high, low = split_terms(small)
                send2 = jnp.concatenate([keep2, high, low], 0)
        token = corner(keep2)
        if more:
            got2 = mix.permute(send2, stage + 1)

    for stage in reversed(range(min(HALVINGS, big_stages))):
        (keep1,) = after(token, keep1)
        other1 = big.permute(keep1, stage)
        other2 = mix.permute(keep2, stage)
        other1, keep1 = after(token, other1, keep1)
        keep1 = join(keep1, other1, big.bits[stage], big.units)
        token = corner(keep1)
        other2, keep2 = after(token, other2, keep2)
        keep2 = join(keep2, other2, mix.bits[stage], mix.units)
        token = corner(keep2)

    unit = lambda arr, u: arr[u * width:(u + 1) * width]
    peer1 = core_swap(keep1)
    peer2 = core_swap(keep2)
    is0 = core == 0
    lo1, hi1 = jnp.where(is0, keep1, peer1), jnp.where(is0, peer1, keep1)
    down_grad = jnp.concatenate([lo1[:2 * width], hi1[:2 * width]], 0).astype(F32)
    up_grad = jnp.concatenate([unit(lo1, 2), unit(lo1, 3), unit(hi1, 2), unit(hi1, 3)], 1).astype(F32)
    lo2, hi2 = jnp.where(is0, keep2, peer2), jnp.where(is0, peer2, keep2)
    qkv_grad = jnp.concatenate([unit(lo2, 0), unit(lo2, 1), unit(hi2, 0)], 1).astype(F32)
    out_grad = unit(hi2, 1).astype(F32)

    shown = []
    for p in range(count):
        value = back[0]
        for k_at in range(1, nseq):
            value = jnp.where((seq ^ p) == k_at, back[k_at], value)
        shown.append(value)
    layer_out = jnp.stack([value[:local] for value in shown])
    input_grad = jnp.stack([value[local:] for value in shown])
    return (
        layer_out,
        input_grad,
        qkv_grad,
        small[6],
        small[7],
        out_grad,
        small[5],
        small[3],
        small[4],
        up_grad,
        small[8:12].reshape(-1),
        down_grad,
        small[2],
        small[0],
        small[1],
    )


def solution(mesh):
    split = P("dp", "seq", None)
    return jax.shard_map(
        body,
        mesh=mesh,
        in_specs=(split, P("dp")) + (P(),) * 13 + (split,),
        out_specs=(split, split) + (P(),) * 13,
        check_vma=False,
    )
```

```python
import functools
import math

import jax
import jax.numpy as jnp
from jax import lax
from jax.experimental import pallas as pl
from jax.experimental.pallas import tpu as pltpu
from jax.sharding import PartitionSpec as P

HEADS = 12
EPS = 1e-12
BF = jnp.bfloat16
F32 = jnp.float32
VMEM_LIMIT = 60 * 1024 * 1024
LOG2E = math.log2(math.e)
S_SEQ, S_LEN, S_CORE, S_BITS = range(4)
ORDER = ((0, 1, 2), (1, 2, 0), (2, 0, 1))
COLORS = 3
LEAF = 16


def dot_nn(left, right):
    return lax.dot_general(left, right, (((1,), (0,)), ((), ())), preferred_element_type=F32)


def dot_nt(left, right):
    return lax.dot_general(left, right, (((1,), (1,)), ((), ())), preferred_element_type=F32)


def dot_tn(left, right):
    return lax.dot_general(left, right, (((0,), (0,)), ((), ())), preferred_element_type=F32)


def params(flag=None):
    return pltpu.CompilerParams(vmem_limit_bytes=VMEM_LIMIT)


def cost(flops, nbytes, trans=0):
    return pl.CostEstimate(flops=int(flops), bytes_accessed=int(nbytes), transcendentals=int(trans))


def full(shape):
    zeros = (0,) * len(shape)
    return pl.BlockSpec(shape, lambda *_: zeros)


def shape_of(shape, dtype):
    return jax.ShapeDtypeStruct(shape, dtype)


def attn_fwd_body(sc, h0, h1, h2, h3, wq, wk, wv, qb, vb, wo, ob, gain, shift,
                  hlc, q_o, k_o, v_o, lse_o, n1_o, r1_o, acc, lse_s):
    step = pl.program_id(0)
    steps = pl.num_programs(0)
    local, width = h0.shape
    rows = hlc.shape[0]
    head = wq.shape[1] // 2
    wide = 2 * head

    @pl.when(step == 0)
    def _():
        for at, ref in enumerate((h0, h1, h2, h3)):
            hlc[at * local:(at + 1) * local, width:2 * width] = ref[...]
        acc[...] = jnp.zeros_like(acc)
        lse_s[...] = jnp.zeros_like(lse_s)

    x = hlc[:, width:2 * width]
    w = jnp.concatenate([wq[...], wk[...], wv[...]], axis=1)
    both = dot_nn(x, w)
    q_o[...] = (both[:, :wide] + qb[...]).astype(BF)
    k_o[...] = both[:, wide:2 * wide].astype(BF)
    v_o[...] = (both[:, 2 * wide:] + vb[...]).astype(BF)
    k = k_o[...]
    v = v_o[...]
    key = lax.broadcasted_iota(jnp.int32, (1, rows), 1)
    place = ((key // local) ^ sc[S_SEQ]) * local + key % local
    mask = jnp.where(place < sc[S_LEN], 0.0, -1e30).astype(F32)
    scale = head ** (-0.5) * LOG2E
    chunk = rows
    lane = lax.broadcasted_iota(jnp.int32, (chunk, wide), 1)
    lane_l = lax.broadcasted_iota(jnp.int32, (chunk, lse_s.shape[1]), 1)
    for part in range(rows // chunk):
        span = pl.ds(part * chunk, chunk)
        q = q_o[span, :]
        outs = []
        tops = []
        for h in range(2):
            mine = (lane >= h * head) & (lane < (h + 1) * head)
            qh = jnp.where(mine, q, jnp.zeros_like(q))
            s = dot_nt(qh, k) * scale + mask
            top = jnp.max(s, -1, keepdims=True)
            e = jnp.exp2(s - top)
            total = jnp.sum(e, -1, keepdims=True)
            pv = dot_nn(e.astype(BF), v)
            outs.append(pv / total)
            tops.append(top + jnp.log2(total))
        ctx = jnp.where(lane < head, outs[0], outs[1]).astype(BF)
        hlc[span, pl.ds(pl.multiple_of(2 * width + step * wide, wide), wide)] = ctx
        acc[span, :] += dot_nn(ctx, wo[...])
        old = lse_s[span, :]
        old = jnp.where(lane_l == 2 * step, tops[0], old)
        lse_s[span, :] = jnp.where(lane_l == 2 * step + 1, tops[1], old)

    @pl.when(step == steps - 1)
    def _():
        lse_o[...] = jnp.transpose(lse_s[...])[:lse_o.shape[0], :]

        @pl.loop(0, rows // local)
        def _(part):
            span = pl.ds(pl.multiple_of(part * local, local), local)
            val = hlc[span, width:2 * width].astype(F32) + (acc[span, :] + ob[...])
            cen = val - jnp.mean(val, -1, keepdims=True)
            r = lax.rsqrt(jnp.mean(cen * cen, -1, keepdims=True) + EPS)
            n = cen * r
            n1_o[span, :] = n
            r1_o[span, :] = jnp.broadcast_to(r, (local, r1_o.shape[1]))
            hlc[span, :width] = (n * gain[...] + shift[...]).astype(BF)


def attn_fwd(sc, blocks, qkv_w, qb, vb, out_w, ob, gain, shift):
    local, width = blocks[0].shape
    rows = local * len(blocks)
    pairs = HEADS // 2
    wide = width // pairs
    row = lambda i, s: (0, i)
    grid = pltpu.PrefetchScalarGridSpec(
        num_scalar_prefetch=1,
        grid=(pairs,),
        in_specs=[full((local, width))] * 4 + [
            pl.BlockSpec((width, wide), lambda i, s: (0, i)),
            pl.BlockSpec((width, wide), lambda i, s: (0, pairs + i)),
            pl.BlockSpec((width, wide), lambda i, s: (0, 2 * pairs + i)),
            pl.BlockSpec((1, wide), row),
            pl.BlockSpec((1, wide), row),
            pl.BlockSpec((wide, width), lambda i, s: (i, 0)),
            full((1, width)), full((1, width)), full((1, width)),
        ],
        out_specs=[
            full((rows, 3 * width)),
            pl.BlockSpec((rows, wide), row),
            pl.BlockSpec((rows, wide), row),
            pl.BlockSpec((rows, wide), row),
            full((16, rows)),
            full((rows, width)),
            full((rows, 128)),
        ],
        scratch_shapes=[pltpu.VMEM((rows, width), F32), pltpu.VMEM((rows, 128), F32)],
    )
    wide_bf = shape_of((rows, width), BF)
    return pl.pallas_call(
        attn_fwd_body,
        grid_spec=grid,
        out_shape=[shape_of((rows, 3 * width), BF), wide_bf, wide_bf, wide_bf, shape_of((16, rows), F32),
                   shape_of((rows, width), F32), shape_of((rows, 128), F32)],
        compiler_params=params(),
        cost_estimate=cost(2 * rows * width * width * 4 + 4 * rows * rows * width, 12 * rows * width + 8 * width * width,
                           HEADS * rows * rows),
        name="attn_fwd",
    )(sc, *blocks, qkv_w, qkv_w, qkv_w, qb, vb, out_w, ob, gain, shift)


def start(copies):
    for copy in copies:
        copy.start()


def wait(copies):
    for copy in copies:
        copy.wait()


def ffn_body(sc, hlc, n1_h, wu_h, wd_h, wo_h, r1, c0, c1, c2, c3, gain1, shift1, ub, db, gain2, shift2,
             act_o, send_o, dup_o, dsend_o, lo_o, dres_o, dattn_o, dctx_o, stat_o,
             low, n1, wu, wd, wo, act, slope, acc, dsec, dffn, dup, sem_in, sem_w, sem_out):
    local, width = c0.shape
    rows, inner = act.shape
    tile = width
    steps = inner // tile
    side = inner // 2
    core = sc[S_CORE]
    mine = pl.ds(pl.multiple_of(core * side, side), side)
    theirs = pl.ds(pl.multiple_of((1 - core) * side, side), side)

    def cols(j):
        return pl.ds(pl.multiple_of(j * tile, tile), tile)

    def wu_copy(j):
        return pltpu.make_async_copy(wu_h.at[:, cols(j)], wu.at[:, cols(j)], sem_w.at[0, j])

    def wd_copy(j):
        return pltpu.make_async_copy(wd_h.at[cols(j), :], wd.at[cols(j), :], sem_w.at[1, j])

    low_copy = pltpu.make_async_copy(hlc.at[:, pl.ds(0, width)], low, sem_in.at[0])
    n1_copy = pltpu.make_async_copy(n1_h, n1, sem_in.at[1])
    wo_copy = pltpu.make_async_copy(wo_h, wo, sem_in.at[2])
    low_copy.start()
    for j in range(steps):
        wu_copy(j).start()
        wd_copy(j).start()
    start([n1_copy, wo_copy])
    low_copy.wait()
    stat_o[...] = jnp.zeros_like(stat_o)

    def forward(j, _):
        wu_copy(j).wait()
        wd_copy(j).wait()
        up = dot_nn(low[...], wu[:, cols(j)]) + ub[:, cols(j)]
        cdf = 0.5 * (1.0 + lax.erf(up * (2.0 ** -0.5)))
        bell = jnp.exp2(up * up * (-0.5 * LOG2E)) * ((2.0 * math.pi) ** -0.5)
        val = (up * cdf).astype(BF)
        act[:, cols(j)] = val
        slope[:, cols(j)] = (cdf + up * bell).astype(BF)
        term = dot_nn(val, wd[cols(j), :])

        @pl.when(j == 0)
        def _():
            acc[...] = term

        @pl.when(j > 0)
        def _():
            acc[...] += term
        return 0

    lax.fori_loop(0, steps, forward, 0)
    act_out = [pltpu.make_async_copy(act.at[:, mine], act_o, sem_out.at[0]),
               pltpu.make_async_copy(act.at[:, theirs], send_o.at[:, pl.ds(0, side)], sem_out.at[1])]
    start(act_out)
    n1_copy.wait()
    for at, cot in enumerate((c0, c1, c2, c3)):
        span = pl.ds(at * local, local)
        first = n1[span, :] * gain1[...] + shift1[...]
        val = first + (acc[span, :] + db[...])
        cen = val - jnp.mean(val, -1, keepdims=True)
        r = lax.rsqrt(jnp.mean(cen * cen, -1, keepdims=True) + EPS)
        n = cen * r
        lo_o[span, :] = (n * gain2[...] + shift2[...]).astype(BF)
        dy = cot[...].astype(F32)
        dn = dy * gain2[...]
        ds = r * (dn - jnp.mean(dn, -1, keepdims=True) - n * jnp.mean(dn * n, -1, keepdims=True))
        dsec[span, :] = ds
        dlow = ds.astype(BF)
        dffn[span, :] = dlow
        stat_o[0:1, :] += jnp.sum(dy * n, 0, keepdims=True)
        stat_o[1:2, :] += jnp.sum(dy, 0, keepdims=True)
        stat_o[2:3, :] += jnp.sum(dlow.astype(F32), 0, keepdims=True)
    dffn_out = pltpu.make_async_copy(dffn, send_o.at[:, pl.ds(side, width)], sem_out.at[2])
    dffn_out.start()

    def backward(j, _):
        dact = dot_nt(dffn[...], wd[cols(j), :])
        val = (dact * slope[:, cols(j)].astype(F32)).astype(BF)
        dup[:, cols(j)] = val
        stat_o[pl.ds(8 + j, 1), :] = jnp.sum(val.astype(F32), 0, keepdims=True)
        dsec[...] += dot_nt(val, wu[:, cols(j)])
        return 0

    lax.fori_loop(0, steps, backward, 0)
    dup_out = [pltpu.make_async_copy(dup.at[:, mine], dup_o, sem_out.at[3]),
               pltpu.make_async_copy(dup.at[:, theirs], dsend_o, sem_out.at[4])]
    start(dup_out)
    wo_copy.wait()

    @pl.loop(0, rows // local)
    def _(at):
        span = pl.ds(pl.multiple_of(at * local, local), local)
        dfirst = dsec[span, :]
        n = n1[span, :]
        dn = dfirst * gain1[...]
        r = r1[span, 0:1]
        dres = r * (dn - jnp.mean(dn, -1, keepdims=True) - n * jnp.mean(dn * n, -1, keepdims=True))
        dres_o[span, :] = dres
        dlow = dres.astype(BF)
        dattn_o[span, :] = dlow
        stat_o[3:4, :] += jnp.sum(dfirst * n, 0, keepdims=True)
        stat_o[4:5, :] += jnp.sum(dfirst, 0, keepdims=True)
        stat_o[5:6, :] += jnp.sum(dlow.astype(F32), 0, keepdims=True)

    dctx_o[...] = dot_nt(dattn_o[...], wo[...]).astype(BF)
    wait(act_out + [dffn_out] + dup_out)


def ffn(sc, hlc, n1, r1, wu, wd, wo, cots, gain1, shift1, ub, db, gain2, shift2):
    rows, width = n1.shape
    inner = wu.shape[1]
    steps = inner // width
    smem = pl.BlockSpec(memory_space=pltpu.SMEM)
    anywhere = pl.BlockSpec(memory_space=pl.ANY)
    vmem = pl.BlockSpec(memory_space=pltpu.VMEM)
    half = shape_of((rows, inner // 2), BF)
    wide = shape_of((rows, width), BF)
    return pl.pallas_call(
        ffn_body,
        in_specs=[smem] + [anywhere] * 5 + [vmem] * 11,
        out_specs=[anywhere] * 4 + [vmem] * 5,
        out_shape=[half, shape_of((rows, inner // 2 + width), BF), half, half, wide, shape_of((rows, width), F32),
                   wide, wide, shape_of((16, width), F32)],
        scratch_shapes=[pltpu.VMEM((rows, width), BF), pltpu.VMEM((rows, width), F32), pltpu.VMEM((width, inner), BF),
                        pltpu.VMEM((inner, width), BF), pltpu.VMEM((width, width), BF), pltpu.VMEM((rows, inner), BF),
                        pltpu.VMEM((rows, inner), BF), pltpu.VMEM((rows, width), F32), pltpu.VMEM((rows, width), F32),
                        pltpu.VMEM((rows, width), BF), pltpu.VMEM((rows, inner), BF), pltpu.SemaphoreType.DMA((3,)),
                        pltpu.SemaphoreType.DMA((2, steps)), pltpu.SemaphoreType.DMA((5,))],
        compiler_params=params(),
        cost_estimate=cost(8 * rows * width * inner, 4 * width * inner + 6 * rows * inner, 2 * rows * inner),
        name="ffn",
    )(sc, hlc, n1, wu, wd, wo, r1, *cots, gain1, shift1, ub, db, gain2, shift2)


def split_terms(value):
    high = value.astype(BF)
    return high, (value - high.astype(F32)).astype(BF)


def attn_bwd_body(sc, q_r, k_r, v_r, g_r, lse, wq, wk, wv, base, da_r, stat, lo, *refs, first, last):
    if first:
        dq_o, dk_o, dv_o, one_o, two_o, small_o, acc = refs
    else:
        dq_o, dk_o, dv_o, one_o, two_o, small_o, terms_o, i0, i1, i2, i3, acc = refs[5:]
    step = pl.program_id(0)
    steps = pl.num_programs(0)
    rows, wide = q_r.shape
    head = wide // 2
    local = rows // 4
    scale = head ** (-0.5)
    pair = step if first else step + steps
    q = q_r[...]
    g = g_r[...]
    k = k_r[...]
    v = v_r[...]
    lane = lax.broadcasted_iota(jnp.int32, (rows, wide), 1)
    key = lax.broadcasted_iota(jnp.int32, (rows, 1), 0)
    place = ((key // local) ^ sc[S_SEQ]) * local + key % local
    mask = jnp.where(place < sc[S_LEN], 0.0, -1e30).astype(F32)
    dks, dvs, dqs = [], [], []
    for h in range(2):
        mine = (lane >= h * head) & (lane < (h + 1) * head)
        qh = jnp.where(mine, q, jnp.zeros_like(q))
        gh = jnp.where(mine, g, jnp.zeros_like(g))
        row = lse[pl.ds(2 * pair + h, 1), :]
        s = dot_nt(k, qh) * (scale * LOG2E) + mask
        p = jnp.exp2(s - row)
        dp = dot_nt(v, gh)
        delta = jnp.sum(p * dp, 0, keepdims=True)
        dvs.append(dot_nn(p.astype(BF), g))
        ds = (p * (dp - delta)).astype(BF)
        dks.append(dot_nn(ds, q))
        dqs.append(dot_tn(ds, k))
    low = lane < head
    dq_o[...] = (jnp.where(low, dqs[0], dqs[1]) * scale).astype(BF)
    dk_o[...] = (jnp.where(low, dks[0], dks[1]) * scale).astype(BF)
    dv_o[...] = jnp.where(low, dvs[0], dvs[1]).astype(BF)
    dqv = dq_o[...]
    dkv = dk_o[...]
    dvv = dv_o[...]
    here = pl.ds(pl.multiple_of(pair * wide, wide), wide)

    @pl.when(step == 0)
    def _():
        small_o[...] = stat[...]

    small_o[6:7, here] = jnp.sum(dqv.astype(F32), 0, keepdims=True)
    small_o[7:8, here] = jnp.sum(dvv.astype(F32), 0, keepdims=True)

    @pl.when(sc[S_CORE] == 0)
    def _():
        one_o[...] = dv_o[...]
        two_o[...] = da_r[...]

    @pl.when(sc[S_CORE] != 0)
    def _():
        one_o[...] = dq_o[...]
        two_o[...] = dk_o[...]

    three = jnp.concatenate([dqv, dkv, dvv], axis=1)
    w = jnp.concatenate([wq[...], wk[...], wv[...]], axis=1)
    term = dot_nt(three, w)

    @pl.when(step == 0)
    def _():
        acc[...] = base[...] + term

    @pl.when(step > 0)
    def _():
        acc[...] += term

    if last:
        @pl.when(step == steps - 1)
        def _():
            for at, ref in enumerate((i0, i1, i2, i3)):
                ref[0:local, :] = lo[at * local:(at + 1) * local, :]
                ref[local:2 * local, :] = acc[pl.ds(at * local, local), :].astype(BF)
            high, rest = split_terms(small_o[...])
            terms_o[0:16, :] = high
            terms_o[16:32, :] = rest


def attn_bwd(sc, q, k, v, g, lse, qkv_w, base, dattn, stat, lo, into):
    rows, width = q.shape
    pairs = HEADS // 2
    wide = width // pairs
    first = not into
    steps = pairs // 2
    off = 0 if first else steps
    col = pl.BlockSpec((rows, wide), lambda i, s: (0, off + i))
    block = full((2 * (rows // 4), width))
    grid = pltpu.PrefetchScalarGridSpec(
        num_scalar_prefetch=1,
        grid=(steps,),
        in_specs=[col, col, col, col, full(lse.shape),
                  pl.BlockSpec((width, wide), lambda i, s: (0, off + i)),
                  pl.BlockSpec((width, wide), lambda i, s: (0, pairs + off + i)),
                  pl.BlockSpec((width, wide), lambda i, s: (0, 2 * pairs + off + i)),
                  full((rows, width)), col, full((16, width)), full((rows, width))]
        + [pl.BlockSpec(memory_space=pl.ANY)] * len(into),
        out_specs=[col] * 5 + [full((16, width))]
        + ([full((rows, width))] if first else [full((32, width))] + [block] * 4),
        scratch_shapes=[] if first else [pltpu.VMEM((rows, width), F32)],
    )
    wide_bf = shape_of((rows, width), BF)
    outs = [wide_bf] * 5 + [shape_of((16, width), F32)]
    if first:
        outs += [shape_of((rows, width), F32)]
    else:
        outs += [shape_of((32, width), BF)] + [shape_of((rows // 2, width), BF)] * 4
    return pl.pallas_call(
        functools.partial(attn_bwd_body, first=first, last=not first),
        grid_spec=grid,
        out_shape=outs,
        input_output_aliases={13 + i: i for i in range(len(into))},
        compiler_params=params(),
        cost_estimate=cost(3 * rows * width * width + 5 * rows * rows * width, 6 * rows * width + 3 * width * width,
                           HEADS * rows * rows // 2),
        name="attn_bwd",
    )(sc, q, k, v, g, lse, qkv_w, qkv_w, qkv_w, base, dattn, stat, lo, *into)


def cut_out(sc, buf, u, sends, keeps, sems):
    copies = []
    third = buf.shape[1] // COLORS
    half = third // 2
    for c in range(COLORS):
        bit = sc[S_BITS + ORDER[c][0]]
        for at, (ref, pick) in enumerate(((sends[c], 1 - bit), (keeps[c], bit))):
            src = buf.at[u, pl.ds(pl.multiple_of(c * third + pick * half, half), half), :]
            copies.append(pltpu.make_async_copy(src, ref.at[pl.ds(u * half, half), :], sems.at[u, 2 * c + at]))
    start(copies)
    return copies


def wgrad_body(sc, act_h, send_h, peer_h, hlc, hlcp, dup_h, dupp_h, s0, s1, s2, k0, k1, k2,
               act, actp, dffn, low, lowp, dup, dupp, buf, sem_in, sem_out):
    side = act.shape[1]
    width = dffn.shape[1]
    loads = [
        pltpu.make_async_copy(act_h, act, sem_in.at[0]),
        pltpu.make_async_copy(send_h.at[:, pl.ds(side, width)], dffn, sem_in.at[1]),
        pltpu.make_async_copy(peer_h, actp, sem_in.at[2]),
        pltpu.make_async_copy(hlc.at[:, pl.ds(0, width)], low, sem_in.at[3]),
        pltpu.make_async_copy(dup_h, dup, sem_in.at[4]),
        pltpu.make_async_copy(hlcp.at[:, pl.ds(0, width)], lowp, sem_in.at[5]),
        pltpu.make_async_copy(dupp_h, dupp, sem_in.at[6]),
    ]
    start(loads)
    sends, keeps = (s0, s1, s2), (k0, k1, k2)
    copies = []
    wait(loads[:3])
    for u in range(2):
        at = slice(u * width, (u + 1) * width)
        val = dot_tn(act[:, at], dffn[...]) + dot_tn(actp[:, at], actp[:, side:])
        buf[u] = val.astype(BF)
        copies += cut_out(sc, buf, u, sends, keeps, sem_out)
    wait(loads[3:])
    for u in range(2):
        at = slice(u * width, (u + 1) * width)
        val = dot_tn(low[...], dup[:, at]) + dot_tn(lowp[...], dupp[:, at])
        buf[2 + u] = val.astype(BF)
        copies += cut_out(sc, buf, 2 + u, sends, keeps, sem_out)
    wait(copies)


def wgrad(sc, act, send, peer, hlc, hlcp, dup, dupp):
    rows, side = act.shape
    width = hlc.shape[1] // 3
    units = 4
    half = width // COLORS // 2
    anywhere = pl.BlockSpec(memory_space=pl.ANY)
    part = shape_of((units * half, width), BF)
    return pl.pallas_call(
        wgrad_body,
        in_specs=[pl.BlockSpec(memory_space=pltpu.SMEM)] + [anywhere] * 7,
        out_specs=[anywhere] * 6,
        out_shape=[part] * 6,
        scratch_shapes=[pltpu.VMEM((rows, side), BF), pltpu.VMEM((rows, side + width), BF), pltpu.VMEM((rows, width), BF),
                        pltpu.VMEM((rows, width), BF), pltpu.VMEM((rows, width), BF), pltpu.VMEM((rows, side), BF),
                        pltpu.VMEM((rows, side), BF), pltpu.VMEM((units, width, width), BF),
                        pltpu.SemaphoreType.DMA((7,)), pltpu.SemaphoreType.DMA((units, 6))],
        compiler_params=params(),
        cost_estimate=cost(16 * rows * width * width, 26 * rows * width),
        name="wgrad",
    )(sc, act, send, peer, hlc, hlcp, dup, dupp)


def wgrad_mix_body(sc, hlc, hlcp, dq_h, dk_h, dv_h, da_h, p1_h, p2_h, terms, small, s0, s1, s2, k0, k1, k2, small_o,
                   l1, l1p, l2, l2p, r1, r1p, r2, r2p, buf, sem_in, sem_out):
    width = l1.shape[1]
    core = sc[S_CORE]
    second = pl.ds(pl.multiple_of((1 + core) * width, width), width)
    loads = [
        pltpu.make_async_copy(hlc.at[:, pl.ds(width, width)], l1, sem_in.at[0]),
        pltpu.make_async_copy(hlcp.at[:, pl.ds(width, width)], l1p, sem_in.at[1]),
        pltpu.make_async_copy(p1_h, r1p, sem_in.at[2]),
        pltpu.make_async_copy(hlc.at[:, second], l2, sem_in.at[3]),
        pltpu.make_async_copy(hlcp.at[:, second], l2p, sem_in.at[4]),
        pltpu.make_async_copy(p2_h, r2p, sem_in.at[5]),
    ]
    start(loads)

    @pl.when(core == 0)
    def _():
        start([pltpu.make_async_copy(dq_h, r1, sem_in.at[6]), pltpu.make_async_copy(dk_h, r2, sem_in.at[7])])

    @pl.when(core != 0)
    def _():
        start([pltpu.make_async_copy(dv_h, r1, sem_in.at[6]), pltpu.make_async_copy(da_h, r2, sem_in.at[7])])

    tail = [pltpu.make_async_copy(dq_h, r1, sem_in.at[6]), pltpu.make_async_copy(dk_h, r2, sem_in.at[7])]
    small_o[...] = small[...] + (terms[0:16, :].astype(F32) + terms[16:32, :].astype(F32))
    sends, keeps = (s0, s1, s2), (k0, k1, k2)
    wait(loads[:3] + tail[:1])
    buf[0] = (dot_tn(l1[...], r1[...]) + dot_tn(l1p[...], r1p[...])).astype(BF)
    copies = cut_out(sc, buf, 0, sends, keeps, sem_out)
    wait(loads[3:] + tail[1:])
    buf[1] = (dot_tn(l2[...], r2[...]) + dot_tn(l2p[...], r2p[...])).astype(BF)
    copies += cut_out(sc, buf, 1, sends, keeps, sem_out)
    wait(copies)


def wgrad_mix(sc, hlc, hlcp, dq, dk, dv, da, p1, p2, terms, small):
    rows, width = dq.shape
    units = 2
    half = width // COLORS // 2
    anywhere = pl.BlockSpec(memory_space=pl.ANY)
    vmem = pl.BlockSpec(memory_space=pltpu.VMEM)
    part = shape_of((units * half, width), BF)
    return pl.pallas_call(
        wgrad_mix_body,
        in_specs=[pl.BlockSpec(memory_space=pltpu.SMEM)] + [anywhere] * 8 + [vmem] * 2,
        out_specs=[anywhere] * 6 + [vmem],
        out_shape=[part] * 6 + [shape_of(small.shape, F32)],
        scratch_shapes=[pltpu.VMEM((rows, width), BF)] * 8 + [pltpu.VMEM((units, width, width), BF),
                        pltpu.SemaphoreType.DMA((8,)), pltpu.SemaphoreType.DMA((units, 6))],
        compiler_params=params(),
        cost_estimate=cost(8 * rows * width * width, 20 * rows * width),
        name="wgrad_mix",
    )(sc, hlc, hlcp, dq, dk, dv, da, p1, p2, terms, small)


def add_rows(one, two):
    return (one.astype(F32) + two.astype(F32)).astype(BF)


def fold_body(sc, *refs, units, stage, small):
    keeps, gots = refs[:COLORS], refs[COLORS:2 * COLORS]
    outs = refs[2 * COLORS + small:]
    rows = keeps[0].shape[0] // units
    half = rows // 2
    merged = stage == 2
    for c in range(COLORS):
        bit = sc[S_BITS + (3 if merged else ORDER[c][stage + 1])]
        for u in range(units):
            go = pl.ds(pl.multiple_of(u * rows + (1 - bit) * half, LEAF), half)
            stay = pl.ds(pl.multiple_of(u * rows + bit * half, LEAF), half)
            send, keep = (outs[0], outs[1]) if merged else (outs[c], outs[COLORS + c])
            at = (c * units + u) * half if merged else u * half
            send[at:at + half, :] = add_rows(keeps[c][go, :], gots[c][go, :])
            keep[at:at + half, :] = add_rows(keeps[c][stay, :], gots[c][stay, :])
    if small:
        old, new, send = refs[2 * COLORS], outs[-1], outs[0]
        low = units * rows
        val = old[...] + (gots[0][low:low + 16, :].astype(F32) + gots[0][low + 16:low + 32, :].astype(F32))
        new[...] = val
        high, rest = split_terms(val)
        at = send.shape[0] - 32
        send[at:at + 16, :] = high
        send[at + 16:at + 32, :] = rest


def fold(sc, keeps, gots, small, units, stage):
    rows, width = keeps[0].shape
    vmem = pl.BlockSpec(memory_space=pltpu.VMEM)
    has = small is not None
    extra = 32 if has else 0
    if stage == 2:
        outs = [shape_of((COLORS * rows // 2 + extra, width), BF), shape_of((COLORS * rows // 2, width), BF)]
    else:
        outs = [shape_of((rows // 2 + (extra if c == 0 else 0), width), BF) for c in range(COLORS)]
        outs += [shape_of((rows // 2, width), BF)] * COLORS
    args = list(keeps) + list(gots)
    if has:
        args.append(small)
        outs.append(shape_of(small.shape, F32))
    got = pl.pallas_call(
        functools.partial(fold_body, units=units, stage=stage, small=has),
        out_shape=outs,
        in_specs=[pl.BlockSpec(memory_space=pltpu.SMEM)] + [vmem] * len(args),
        out_specs=[vmem] * len(outs),
        compiler_params=params(),
        cost_estimate=cost(6 * rows * width, 18 * rows * width),
        name="fold",
    )(sc, *args)
    if has:
        small = got[-1]
    if stage == 2:
        return [got[0]], [got[1]], small
    return got[:COLORS], got[COLORS:2 * COLORS], small


def total_body(keep, got, *refs):
    rows = keep.shape[0]
    refs[-1 if len(refs) == 1 else 1][...] = add_rows(keep[...], got[0:rows, :])
    if len(refs) > 1:
        refs[2][...] = refs[0][...] + (
            got[rows:rows + 16, :].astype(F32) + got[rows + 16:rows + 32, :].astype(F32))


def total(keep, got, small):
    vmem = pl.BlockSpec(memory_space=pltpu.VMEM)
    args = [keep, got]
    outs = [shape_of(keep.shape, BF)]
    if small is not None:
        args.append(small)
        outs.append(shape_of(small.shape, F32))
    res = pl.pallas_call(
        total_body,
        out_shape=outs,
        in_specs=[vmem] * len(args),
        out_specs=[vmem] * len(outs),
        compiler_params=params(),
        cost_estimate=cost(keep.size, 6 * keep.size),
        name="total",
    )(*args)
    return res[0], (res[1] if small is not None else None)


def join_body(sc, *refs, units, stage):
    outs = refs[-COLORS:]
    n = (len(refs) - COLORS) // 2
    owns, gots = refs[:n], refs[n:2 * n]
    rows = outs[0].shape[0] // units
    half = rows // 2
    for c in range(COLORS):
        bit = sc[S_BITS + (3 if stage == 3 else ORDER[c][stage])]
        own, got = (owns[0], gots[0]) if n == 1 else (owns[c], gots[c])
        for u in range(units):
            at = (c * units + u) * half if n == 1 else u * half
            outs[c][pl.ds(pl.multiple_of(u * rows + bit * half, LEAF), half), :] = own[at:at + half, :]
            outs[c][pl.ds(pl.multiple_of(u * rows + (1 - bit) * half, LEAF), half), :] = got[at:at + half, :]


def joined(sc, owns, gots, units, stage):
    width = owns[0].shape[1]
    rows = 2 * owns[0].shape[0] // (COLORS if len(owns) == 1 else 1)
    vmem = pl.BlockSpec(memory_space=pltpu.VMEM)
    args = list(owns) + list(gots)
    return pl.pallas_call(
        functools.partial(join_body, units=units, stage=stage),
        out_shape=[shape_of((rows, width), BF)] * COLORS,
        in_specs=[pl.BlockSpec(memory_space=pltpu.SMEM)] + [vmem] * len(args),
        out_specs=[vmem] * COLORS,
        compiler_params=params(),
        cost_estimate=cost(rows * width, 12 * rows * width),
        name="join",
    )(sc, *args)


def final_body(sc, *refs, mixed):
    j = pl.program_id(0)
    ins, outs = refs[:4 * COLORS], refs[4 * COLORS:]
    third = outs[0].shape[0] // COLORS
    half = third // 2

    def write(out, owns, gots):
        for c in range(COLORS):
            bit = sc[S_BITS + ORDER[c][0]]
            out[pl.ds(pl.multiple_of(c * third + bit * half, half), half), :] = owns[c][...].astype(F32)
            out[pl.ds(pl.multiple_of(c * third + (1 - bit) * half, half), half), :] = gots[c][...].astype(F32)

    for side in range(2):
        owns = ins[2 * side * COLORS:(2 * side + 1) * COLORS]
        gots = ins[(2 * side + 1) * COLORS:(2 * side + 2) * COLORS]
        here = (j >= 2) if side else (j < 2)
        if not mixed:
            @pl.when(here)
            def _():
                write(outs[0], owns, gots)
        else:
            other = (j % 2 == 1) & ((sc[S_CORE] == 0) if side else (sc[S_CORE] != 0))

            @pl.when(here & jnp.logical_not(other))
            def _():
                write(outs[0], owns, gots)

            @pl.when(here & other)
            def _():
                write(outs[1], owns, gots)


def final(sc, mine, theirs, first, kind):
    width = mine[0].shape[1]
    half = width // COLORS // 2
    own = pl.BlockSpec((half, width), lambda j, s: (first + jnp.minimum(j, 1), 0))
    far = pl.BlockSpec((half, width), lambda j, s: (first + jnp.maximum(j - 2, 0), 0))

    def place(j, s):
        return jnp.where(j < 2, s[S_CORE], 1 - s[S_CORE]) * 2 + j % 2

    if kind == "rows":
        specs = [pl.BlockSpec((width, width), lambda j, s: (place(j, s), 0))]
        outs = [shape_of((4 * width, width), F32)]
    elif kind == "cols":
        specs = [pl.BlockSpec((width, width), lambda j, s: (0, place(j, s)))]
        outs = [shape_of((width, 4 * width), F32)]
    else:
        specs = [pl.BlockSpec((width, width), lambda j, s: (0, jnp.minimum(place(j, s), 2))), full((width, width))]
        outs = [shape_of((width, 3 * width), F32), shape_of((width, width), F32)]
    grid = pltpu.PrefetchScalarGridSpec(
        num_scalar_prefetch=1,
        grid=(4,),
        in_specs=[own] * (2 * COLORS) + [far] * (2 * COLORS),
        out_specs=specs,
    )
    return pl.pallas_call(
        functools.partial(final_body, mixed=len(outs) == 2),
        grid_spec=grid,
        out_shape=outs,
        compiler_params=params(),
        cost_estimate=cost(4 * width * width, 24 * width * width),
        name="final",
    )(sc, *mine, *theirs)


def after(token, *values):
    return lax.optimization_barrier((token,) + values)[1:]


def corner(value):
    return value[:8, :128]


def body(
    hidden_in,
    lengths,
    qkv_weight,
    query_bias,
    value_bias,
    out_weight,
    out_bias,
    attn_gain,
    attn_shift,
    up_weight,
    up_bias,
    down_weight,
    down_bias,
    ffn_gain,
    ffn_shift,
    cotangent,
):
    count, local, width = hidden_in.shape
    nseq = lax.axis_size("seq")
    ndp = lax.axis_size("dp")
    seq = lax.axis_index("seq")
    dp = lax.axis_index("dp")
    core = dp & 1
    flat = seq * ndp + dp
    members = nseq * ndp
    line = lambda vec: vec.reshape(1, -1)

    axes = [ndp, 2 * ndp]
    mask = 2
    while mask < ndp:
        axes.append(mask)
        mask *= 2
    later = axes[4:]

    def permute(value, mask):
        return lax.ppermute(value, ("seq", "dp"), [(i, i ^ mask) for i in range(members)])

    def over(values, stage):
        if stage == 3:
            return [permute(values[0], axes[3])]
        return [permute(values[c], axes[ORDER[c][stage]]) for c in range(COLORS)]

    def core_swap(value):
        return permute(value, 1)

    holder = jnp.minimum(seq, count - 1)
    own_len = lax.dynamic_index_in_dim(lengths, holder, 0, False)
    own_len = jnp.where(seq < count, own_len, nseq * local)
    bits = [jnp.where((flat & mask) != 0, 1, 0) for mask in axes[:4]]
    sc = jnp.stack([seq, own_len, core] + bits + [core]).astype(jnp.int32)

    def to_holder(value):
        blocks = [lax.dynamic_index_in_dim(value, holder, 0, False)]
        parts = [lax.dynamic_index_in_dim(value, jnp.minimum(seq ^ k, count - 1), 0, False) for k in range(1, nseq)]
        for k in range(1, nseq):
            pairs = [(i, i ^ k) for i in range(nseq) if (i ^ k) < count]
            blocks.append(lax.ppermute(parts[k - 1], "seq", pairs))
        return blocks

    hids = to_holder(hidden_in)
    *hids, cot_in = lax.optimization_barrier(tuple(hids) + (cotangent,))
    cots = to_holder(cot_in)
    cots[0] = jnp.where(seq < count, cots[0], jnp.zeros_like(cots[0]))

    hlc, q, k, v, lse, n1, r1 = attn_fwd(
        sc, hids, qkv_weight, line(query_bias), line(value_bias), out_weight, line(out_bias),
        line(attn_gain), line(attn_shift))
    hlc_p = core_swap(hlc)
    act, send, dup, dup_send, lo, dres, dattn, dctx, stat = ffn(
        sc, hlc, n1, r1, up_weight, down_weight, out_weight, cots, line(attn_gain), line(attn_shift),
        line(up_bias), line(down_bias), line(ffn_gain), line(ffn_shift))
    send_p = core_swap(send)
    dup_p = core_swap(dup_send)
    *part, base = attn_bwd(sc, q, k, v, dctx, lse, qkv_weight, dres, dattn, stat, lo, ())
    send_p, dup_p = after(corner(base), send_p, dup_p)
    got = wgrad(sc, act, send, send_p, hlc, hlc_p, dup, dup_p)
    sends1, keeps1 = got[:COLORS], got[COLORS:]
    gots1 = over(sends1, 0)
    (base,) = after(corner(keeps1[0]), base)
    dq, dk, dv, one, two, small, terms, i0, i1, i2, i3 = attn_bwd(
        sc, q, k, v, dctx, lse, qkv_weight, base, dattn, part[5], lo, tuple(part[:5]))
    one_p, two_p, terms_p = core_swap(one), core_swap(two), core_swap(terms)
    token = corner(terms)

    keeps1 = after(token, *keeps1, *gots1)
    keeps1, gots1 = keeps1[:COLORS], keeps1[COLORS:]
    sends1, keeps1, _ = fold(sc, keeps1, gots1, None, 4, 0)
    gots1 = over(sends1, 1)
    one_p, two_p, terms_p = after(corner(keeps1[0]), one_p, two_p, terms_p)
    *got, small = wgrad_mix(sc, hlc, hlc_p, dq, dk, dv, dattn, one_p, two_p, terms_p, small)
    sends2, keeps2 = list(got[:COLORS]), got[COLORS:]
    high, rest = split_terms(small)
    sends2[0] = jnp.concatenate([sends2[0], high, rest], 0)
    gots2 = over(sends2, 0)
    token = corner(keeps2[0])

    def step(kind, token, keeps, gots, small, units, stage):
        held = [] if small is None else [small]
        vals = after(token, *keeps, *gots, *held)
        n = len(keeps)
        keeps, gots = vals[:n], vals[n:2 * n]
        small = vals[2 * n] if held else None
        if kind == "fold":
            if stage < 3:
                sends, keeps, small = fold(sc, keeps, gots, small, units, stage)
            else:
                whole, small = total(keeps[0], gots[0], small)
                for mask in later:
                    if small is None:
                        whole = add_rows(whole, permute(whole, mask))
                    else:
                        high, rest = split_terms(small)
                        more = permute(jnp.concatenate([whole, high, rest], 0), mask)
                        size = whole.shape[0]
                        whole = add_rows(whole, more[:size])
                        small = small + (more[size:size + 16].astype(F32) + more[size + 16:].astype(F32))
                sends = keeps = [whole]
        else:
            sends = keeps = joined(sc, keeps, gots, units, stage)
        return sends, keeps, small, corner(keeps[0])

    plan = [("fold", 1, 1), ("fold", 2, 0), ("fold", 1, 2), ("fold", 2, 1), ("fold", 1, 3), ("fold", 2, 2),
            ("join", 1, 3), ("fold", 2, 3), ("join", 1, 2), ("join", 2, 3), ("join", 1, 1), ("join", 2, 2),
            ("join", 2, 1)]
    state = {1: (keeps1, gots1, None, 4), 2: (keeps2, gots2, small, 2)}
    far = {}
    for at, (kind, piece, stage) in enumerate(plan):
        keeps, gots, small, units = state[piece]
        sends, keeps, small, token = step(kind, token, keeps, gots, small, units, stage)
        if kind == "fold":
            upcoming = stage + 1 if stage < 3 else 3
        else:
            upcoming = stage - 1
        gots = over(sends, upcoming)
        state[piece] = (keeps, gots, small, units)
        if kind == "join" and stage == 1:
            far[piece] = [core_swap(value) for value in keeps]
        if at == 0:
            blocks = after(token, i0, i1, i2, i3)
            back = [blocks[0]]
            for k_at in range(1, nseq):
                pairs = [(i, i ^ k_at) for i in range(nseq) if i < count]
                back.append(lax.ppermute(blocks[k_at], "seq", pairs))

    keeps1, gots1 = state[1][:2]
    vals = after(token, *keeps1, *gots1)
    keeps1, gots1 = vals[:COLORS], vals[COLORS:]
    far1 = far[1] + [core_swap(value) for value in gots1]
    back = after(corner(gots1[0]), *back)
    shown = []
    for p in range(count):
        value = back[0]
        for k_at in range(1, nseq):
            value = jnp.where((seq ^ p) == k_at, back[k_at], value)
        shown.append(value)
    layer_out = jnp.stack([value[:local] for value in shown])
    input_grad = jnp.stack([value[local:] for value in shown])
    mine1 = list(keeps1) + list(gots1)
    (down_grad,) = final(sc, mine1, far1, 0, "rows")
    (up_grad,) = final(sc, mine1, far1, 2, "cols")
    keeps2, gots2, small, _ = state[2]
    vals = after(corner(up_grad), corner(down_grad), *keeps2, *gots2)[1:]
    keeps2, gots2 = vals[:COLORS], vals[COLORS:]
    far2 = far[2] + [core_swap(value) for value in gots2]
    qkv_grad, out_grad = final(sc, list(keeps2) + list(gots2), far2, 0, "mixed")
    return (
        layer_out,
        input_grad,
        qkv_grad,
        small[6],
        small[7],
        out_grad,
        small[5],
        small[3],
        small[4],
        up_grad,
        small[8:12].reshape(-1),
        down_grad,
        small[2],
        small[0],
        small[1],
    )


def solution(mesh):
    split = P("dp", "seq", None)
    return jax.shard_map(
        body,
        mesh=mesh,
        in_specs=(split, P("dp")) + (P(),) * 13 + (split,),
        out_specs=(split, split) + (P(),) * 13,
        check_vma=False,
    )
```

```python
import functools
import math

import jax
import jax.numpy as jnp
from jax import lax
from jax.experimental import pallas as pl
from jax.experimental.pallas import tpu as pltpu
from jax.sharding import PartitionSpec as P

HEADS = 12
EPS = 1e-12
BF = jnp.bfloat16
F32 = jnp.float32
VMEM_LIMIT = 60 * 1024 * 1024
LOG2E = math.log2(math.e)
S_SEQ, S_LEN, S_CORE, S_BITS = range(4)
ORDER = ((0, 1, 2), (1, 2, 0), (2, 0, 1))
COLORS = 3
LEAF = 16


def dot_nn(left, right):
    return lax.dot_general(left, right, (((1,), (0,)), ((), ())), preferred_element_type=F32)


def dot_nt(left, right):
    return lax.dot_general(left, right, (((1,), (1,)), ((), ())), preferred_element_type=F32)


def dot_tn(left, right):
    return lax.dot_general(left, right, (((0,), (0,)), ((), ())), preferred_element_type=F32)


def params(flag=None):
    return pltpu.CompilerParams(vmem_limit_bytes=VMEM_LIMIT)


def cost(flops, nbytes, trans=0):
    return pl.CostEstimate(flops=int(flops), bytes_accessed=int(nbytes), transcendentals=int(trans))


def full(shape):
    zeros = (0,) * len(shape)
    return pl.BlockSpec(shape, lambda *_: zeros)


def shape_of(shape, dtype):
    return jax.ShapeDtypeStruct(shape, dtype)


def attn_fwd_body(sc, h0, h1, h2, h3, wq, wk, wv, qb, vb, wo, ob, gain, shift,
                  hlc, q_o, k_o, v_o, lse_o, n1_o, r1_o, acc, lse_s):
    step = pl.program_id(0)
    steps = pl.num_programs(0)
    local, width = h0.shape
    rows = hlc.shape[0]
    head = wq.shape[1] // 2
    wide = 2 * head

    @pl.when(step == 0)
    def _():
        for at, ref in enumerate((h0, h1, h2, h3)):
            hlc[at * local:(at + 1) * local, width:2 * width] = ref[...]
        acc[...] = jnp.zeros_like(acc)
        lse_s[...] = jnp.zeros_like(lse_s)

    x = hlc[:, width:2 * width]
    w = jnp.concatenate([wq[...], wk[...], wv[...]], axis=1)
    both = dot_nn(x, w)
    q_o[...] = (both[:, :wide] + qb[...]).astype(BF)
    k_o[...] = both[:, wide:2 * wide].astype(BF)
    v_o[...] = (both[:, 2 * wide:] + vb[...]).astype(BF)
    k = k_o[...]
    v = v_o[...]
    key = lax.broadcasted_iota(jnp.int32, (1, rows), 1)
    place = ((key // local) ^ sc[S_SEQ]) * local + key % local
    mask = jnp.where(place < sc[S_LEN], 0.0, -1e30).astype(F32)
    scale = head ** (-0.5) * LOG2E
    chunk = rows
    lane = lax.broadcasted_iota(jnp.int32, (chunk, wide), 1)
    lane_l = lax.broadcasted_iota(jnp.int32, (chunk, lse_s.shape[1]), 1)
    for part in range(rows // chunk):
        span = pl.ds(part * chunk, chunk)
        q = q_o[span, :]
        outs = []
        tops = []
        for h in range(2):
            mine = (lane >= h * head) & (lane < (h + 1) * head)
            qh = jnp.where(mine, q, jnp.zeros_like(q))
            s = dot_nt(qh, k) * scale + mask
            top = jnp.max(s, -1, keepdims=True)
            e = jnp.exp2(s - top)
            total = jnp.sum(e, -1, keepdims=True)
            pv = dot_nn(e.astype(BF), v)
            outs.append(pv / total)
            tops.append(top + jnp.log2(total))
        ctx = jnp.where(lane < head, outs[0], outs[1]).astype(BF)
        hlc[span, pl.ds(pl.multiple_of(2 * width + step * wide, wide), wide)] = ctx
        acc[span, :] += dot_nn(ctx, wo[...])
        old = lse_s[span, :]
        old = jnp.where(lane_l == 2 * step, tops[0], old)
        lse_s[span, :] = jnp.where(lane_l == 2 * step + 1, tops[1], old)

    @pl.when(step == steps - 1)
    def _():
        lse_o[...] = jnp.transpose(lse_s[...])[:lse_o.shape[0], :]

        @pl.loop(0, rows // local)
        def _(part):
            span = pl.ds(pl.multiple_of(part * local, local), local)
            val = hlc[span, width:2 * width].astype(F32) + (acc[span, :] + ob[...])
            cen = val - jnp.mean(val, -1, keepdims=True)
            r = lax.rsqrt(jnp.mean(cen * cen, -1, keepdims=True) + EPS)
            n = cen * r
            n1_o[span, :] = n
            r1_o[span, :] = jnp.broadcast_to(r, (local, r1_o.shape[1]))
            hlc[span, :width] = (n * gain[...] + shift[...]).astype(BF)


def attn_fwd(sc, blocks, qkv_w, qb, vb, out_w, ob, gain, shift):
    local, width = blocks[0].shape
    rows = local * len(blocks)
    pairs = HEADS // 2
    wide = width // pairs
    row = lambda i, s: (0, i)
    grid = pltpu.PrefetchScalarGridSpec(
        num_scalar_prefetch=1,
        grid=(pairs,),
        in_specs=[full((local, width))] * 4 + [
            pl.BlockSpec((width, wide), lambda i, s: (0, i)),
            pl.BlockSpec((width, wide), lambda i, s: (0, pairs + i)),
            pl.BlockSpec((width, wide), lambda i, s: (0, 2 * pairs + i)),
            pl.BlockSpec((1, wide), row),
            pl.BlockSpec((1, wide), row),
            pl.BlockSpec((wide, width), lambda i, s: (i, 0)),
            full((1, width)), full((1, width)), full((1, width)),
        ],
        out_specs=[
            full((rows, 3 * width)),
            pl.BlockSpec((rows, wide), row),
            pl.BlockSpec((rows, wide), row),
            pl.BlockSpec((rows, wide), row),
            full((16, rows)),
            full((rows, width)),
            full((rows, 128)),
        ],
        scratch_shapes=[pltpu.VMEM((rows, width), F32), pltpu.VMEM((rows, 128), F32)],
    )
    wide_bf = shape_of((rows, width), BF)
    return pl.pallas_call(
        attn_fwd_body,
        grid_spec=grid,
        out_shape=[shape_of((rows, 3 * width), BF), wide_bf, wide_bf, wide_bf, shape_of((16, rows), F32),
                   shape_of((rows, width), F32), shape_of((rows, 128), F32)],
        compiler_params=params(),
        cost_estimate=cost(2 * rows * width * width * 4 + 4 * rows * rows * width, 12 * rows * width + 8 * width * width,
                           HEADS * rows * rows),
        name="attn_fwd",
    )(sc, *blocks, qkv_w, qkv_w, qkv_w, qb, vb, out_w, ob, gain, shift)


def start(copies):
    for copy in copies:
        copy.start()


def wait(copies):
    for copy in copies:
        copy.wait()


def ffn_body(sc, hlc, n1_h, wu_h, wd_h, wo_h, r1, c0, c1, c2, c3, gain1, shift1, ub, db, gain2, shift2,
             act_o, send_o, dup_o, dsend_o, lo_o, dres_o, dattn_o, dctx_o, stat_o,
             low, n1, wu, wd, wo, act, slope, acc, dsec, dffn, dup, sem_in, sem_w, sem_out):
    local, width = c0.shape
    rows, inner = act.shape
    tile = width
    steps = inner // tile
    side = inner // 2
    core = sc[S_CORE]
    mine = pl.ds(pl.multiple_of(core * side, side), side)
    theirs = pl.ds(pl.multiple_of((1 - core) * side, side), side)

    def cols(j):
        return pl.ds(pl.multiple_of(j * tile, tile), tile)

    def wu_copy(j):
        return pltpu.make_async_copy(wu_h.at[:, cols(j)], wu.at[:, cols(j)], sem_w.at[0, j])

    def wd_copy(j):
        return pltpu.make_async_copy(wd_h.at[cols(j), :], wd.at[cols(j), :], sem_w.at[1, j])

    low_copy = pltpu.make_async_copy(hlc.at[:, pl.ds(0, width)], low, sem_in.at[0])
    n1_copy = pltpu.make_async_copy(n1_h, n1, sem_in.at[1])
    wo_copy = pltpu.make_async_copy(wo_h, wo, sem_in.at[2])
    low_copy.start()
    for j in range(steps):
        wu_copy(j).start()
        wd_copy(j).start()
    start([n1_copy, wo_copy])
    low_copy.wait()
    stat_o[...] = jnp.zeros_like(stat_o)

    def forward(j, _):
        wu_copy(j).wait()
        wd_copy(j).wait()
        up = dot_nn(low[...], wu[:, cols(j)]) + ub[:, cols(j)]
        cdf = 0.5 * (1.0 + lax.erf(up * (2.0 ** -0.5)))
        bell = jnp.exp2(up * up * (-0.5 * LOG2E)) * ((2.0 * math.pi) ** -0.5)
        val = (up * cdf).astype(BF)
        act[:, cols(j)] = val
        slope[:, cols(j)] = (cdf + up * bell).astype(BF)
        term = dot_nn(val, wd[cols(j), :])

        @pl.when(j == 0)
        def _():
            acc[...] = term

        @pl.when(j > 0)
        def _():
            acc[...] += term
        return 0

    lax.fori_loop(0, steps, forward, 0)
    act_out = [pltpu.make_async_copy(act.at[:, mine], act_o, sem_out.at[0]),
               pltpu.make_async_copy(act.at[:, theirs], send_o.at[:, pl.ds(0, side)], sem_out.at[1])]
    start(act_out)
    n1_copy.wait()
    for at, cot in enumerate((c0, c1, c2, c3)):
        span = pl.ds(at * local, local)
        first = n1[span, :] * gain1[...] + shift1[...]
        val = first + (acc[span, :] + db[...])
        cen = val - jnp.mean(val, -1, keepdims=True)
        r = lax.rsqrt(jnp.mean(cen * cen, -1, keepdims=True) + EPS)
        n = cen * r
        lo_o[span, :] = (n * gain2[...] + shift2[...]).astype(BF)
        dy = cot[...].astype(F32)
        dn = dy * gain2[...]
        ds = r * (dn - jnp.mean(dn, -1, keepdims=True) - n * jnp.mean(dn * n, -1, keepdims=True))
        dsec[span, :] = ds
        dlow = ds.astype(BF)
        dffn[span, :] = dlow
        stat_o[0:1, :] += jnp.sum(dy * n, 0, keepdims=True)
        stat_o[1:2, :] += jnp.sum(dy, 0, keepdims=True)
        stat_o[2:3, :] += jnp.sum(dlow.astype(F32), 0, keepdims=True)
    dffn_out = pltpu.make_async_copy(dffn, send_o.at[:, pl.ds(side, width)], sem_out.at[2])
    dffn_out.start()

    def backward(j, _):
        dact = dot_nt(dffn[...], wd[cols(j), :])
        val = (dact * slope[:, cols(j)].astype(F32)).astype(BF)
        dup[:, cols(j)] = val
        stat_o[pl.ds(8 + j, 1), :] = jnp.sum(val.astype(F32), 0, keepdims=True)
        dsec[...] += dot_nt(val, wu[:, cols(j)])
        return 0

    lax.fori_loop(0, steps, backward, 0)
    dup_out = [pltpu.make_async_copy(dup.at[:, mine], dup_o, sem_out.at[3]),
               pltpu.make_async_copy(dup.at[:, theirs], dsend_o, sem_out.at[4])]
    start(dup_out)
    wo_copy.wait()

    @pl.loop(0, rows // local)
    def _(at):
        span = pl.ds(pl.multiple_of(at * local, local), local)
        dfirst = dsec[span, :]
        n = n1[span, :]
        dn = dfirst * gain1[...]
        r = r1[span, 0:1]
        dres = r * (dn - jnp.mean(dn, -1, keepdims=True) - n * jnp.mean(dn * n, -1, keepdims=True))
        dres_o[span, :] = dres
        dlow = dres.astype(BF)
        dattn_o[span, :] = dlow
        stat_o[3:4, :] += jnp.sum(dfirst * n, 0, keepdims=True)
        stat_o[4:5, :] += jnp.sum(dfirst, 0, keepdims=True)
        stat_o[5:6, :] += jnp.sum(dlow.astype(F32), 0, keepdims=True)

    dctx_o[...] = dot_nt(dattn_o[...], wo[...]).astype(BF)
    wait(act_out + [dffn_out] + dup_out)


def ffn(sc, hlc, n1, r1, wu, wd, wo, cots, gain1, shift1, ub, db, gain2, shift2):
    rows, width = n1.shape
    inner = wu.shape[1]
    steps = inner // width
    smem = pl.BlockSpec(memory_space=pltpu.SMEM)
    anywhere = pl.BlockSpec(memory_space=pl.ANY)
    vmem = pl.BlockSpec(memory_space=pltpu.VMEM)
    half = shape_of((rows, inner // 2), BF)
    wide = shape_of((rows, width), BF)
    return pl.pallas_call(
        ffn_body,
        in_specs=[smem] + [anywhere] * 5 + [vmem] * 11,
        out_specs=[anywhere] * 4 + [vmem] * 5,
        out_shape=[half, shape_of((rows, inner // 2 + width), BF), half, half, wide, shape_of((rows, width), F32),
                   wide, wide, shape_of((16, width), F32)],
        scratch_shapes=[pltpu.VMEM((rows, width), BF), pltpu.VMEM((rows, width), F32), pltpu.VMEM((width, inner), BF),
                        pltpu.VMEM((inner, width), BF), pltpu.VMEM((width, width), BF), pltpu.VMEM((rows, inner), BF),
                        pltpu.VMEM((rows, inner), BF), pltpu.VMEM((rows, width), F32), pltpu.VMEM((rows, width), F32),
                        pltpu.VMEM((rows, width), BF), pltpu.VMEM((rows, inner), BF), pltpu.SemaphoreType.DMA((3,)),
                        pltpu.SemaphoreType.DMA((2, steps)), pltpu.SemaphoreType.DMA((5,))],
        compiler_params=params(),
        cost_estimate=cost(8 * rows * width * inner, 4 * width * inner + 6 * rows * inner, 2 * rows * inner),
        name="ffn",
    )(sc, hlc, n1, wu, wd, wo, r1, *cots, gain1, shift1, ub, db, gain2, shift2)


def split_terms(value):
    high = value.astype(BF)
    return high, (value - high.astype(F32)).astype(BF)


def attn_bwd_body(sc, q_r, k_r, v_r, g_r, lse, wq, wk, wv, base, da_r, stat, lo, *refs, first, last, deps):
    if first:
        dq_o, dk_o, dv_o, one_o, two_o, small_o, acc = refs
    else:
        dq_o, dk_o, dv_o, one_o, two_o, small_o, terms_o, i0, i1, i2, i3, acc = refs[5 + deps:]
    step = pl.program_id(0)
    steps = pl.num_programs(0)
    rows, wide = q_r.shape
    head = wide // 2
    local = rows // 4
    scale = head ** (-0.5)
    pair = step if first else step + steps
    q = q_r[...]
    g = g_r[...]
    k = k_r[...]
    v = v_r[...]
    lane = lax.broadcasted_iota(jnp.int32, (rows, wide), 1)
    key = lax.broadcasted_iota(jnp.int32, (rows, 1), 0)
    place = ((key // local) ^ sc[S_SEQ]) * local + key % local
    mask = jnp.where(place < sc[S_LEN], 0.0, -1e30).astype(F32)
    dks, dvs, dqs = [], [], []
    for h in range(2):
        mine = (lane >= h * head) & (lane < (h + 1) * head)
        qh = jnp.where(mine, q, jnp.zeros_like(q))
        gh = jnp.where(mine, g, jnp.zeros_like(g))
        row = lse[pl.ds(2 * pair + h, 1), :]
        s = dot_nt(k, qh) * (scale * LOG2E) + mask
        p = jnp.exp2(s - row)
        dp = dot_nt(v, gh)
        delta = jnp.sum(p * dp, 0, keepdims=True)
        dvs.append(dot_nn(p.astype(BF), g))
        ds = (p * (dp - delta)).astype(BF)
        dks.append(dot_nn(ds, q))
        dqs.append(dot_tn(ds, k))
    low = lane < head
    dq_o[...] = (jnp.where(low, dqs[0], dqs[1]) * scale).astype(BF)
    dk_o[...] = (jnp.where(low, dks[0], dks[1]) * scale).astype(BF)
    dv_o[...] = jnp.where(low, dvs[0], dvs[1]).astype(BF)
    dqv = dq_o[...]
    dkv = dk_o[...]
    dvv = dv_o[...]
    here = pl.ds(pl.multiple_of(pair * wide, wide), wide)

    @pl.when(step == 0)
    def _():
        small_o[...] = stat[...]

    small_o[6:7, here] = jnp.sum(dqv.astype(F32), 0, keepdims=True)
    small_o[7:8, here] = jnp.sum(dvv.astype(F32), 0, keepdims=True)

    @pl.when(sc[S_CORE] == 0)
    def _():
        one_o[...] = dv_o[...]
        two_o[...] = da_r[...]

    @pl.when(sc[S_CORE] != 0)
    def _():
        one_o[...] = dq_o[...]
        two_o[...] = dk_o[...]

    three = jnp.concatenate([dqv, dkv, dvv], axis=1)
    w = jnp.concatenate([wq[...], wk[...], wv[...]], axis=1)
    term = dot_nt(three, w)

    @pl.when(step == 0)
    def _():
        acc[...] = base[...] + term

    @pl.when(step > 0)
    def _():
        acc[...] += term

    if last:
        @pl.when(step == steps - 1)
        def _():
            for at, ref in enumerate((i0, i1, i2, i3)):
                ref[0:local, :] = lo[at * local:(at + 1) * local, :]
                ref[local:2 * local, :] = acc[pl.ds(at * local, local), :].astype(BF)
            high, rest = split_terms(small_o[...])
            terms_o[0:16, :] = high
            terms_o[16:32, :] = rest


def attn_bwd(sc, q, k, v, g, lse, qkv_w, base, dattn, stat, lo, into, deps=()):
    rows, width = q.shape
    pairs = HEADS // 2
    wide = width // pairs
    first = not into
    steps = pairs // 2
    off = 0 if first else steps
    col = pl.BlockSpec((rows, wide), lambda i, s: (0, off + i))
    block = full((2 * (rows // 4), width))
    grid = pltpu.PrefetchScalarGridSpec(
        num_scalar_prefetch=1,
        grid=(steps,),
        in_specs=[col, col, col, col, full(lse.shape),
                  pl.BlockSpec((width, wide), lambda i, s: (0, off + i)),
                  pl.BlockSpec((width, wide), lambda i, s: (0, pairs + off + i)),
                  pl.BlockSpec((width, wide), lambda i, s: (0, 2 * pairs + off + i)),
                  full((rows, width)), col, full((16, width)), full((rows, width))]
        + [pl.BlockSpec(memory_space=pl.ANY)] * (len(into) + len(deps)),
        out_specs=[col] * 5 + [full((16, width))]
        + ([full((rows, width))] if first else [full((32, width))] + [block] * 4),
        scratch_shapes=[] if first else [pltpu.VMEM((rows, width), F32)],
    )
    wide_bf = shape_of((rows, width), BF)
    outs = [wide_bf] * 5 + [shape_of((16, width), F32)]
    if first:
        outs += [shape_of((rows, width), F32)]
    else:
        outs += [shape_of((32, width), BF)] + [shape_of((rows // 2, width), BF)] * 4
    return pl.pallas_call(
        functools.partial(attn_bwd_body, first=first, last=not first, deps=len(deps)),
        grid_spec=grid,
        out_shape=outs,
        input_output_aliases={13 + i: i for i in range(len(into))},
        compiler_params=params(),
        cost_estimate=cost(3 * rows * width * width + 5 * rows * rows * width, 6 * rows * width + 3 * width * width,
                           HEADS * rows * rows // 2),
        name="attn_bwd",
    )(sc, q, k, v, g, lse, qkv_w, qkv_w, qkv_w, base, dattn, stat, lo, *into, *deps)


def cut_out(sc, buf, u, sends, keeps, sems):
    copies = []
    third = buf.shape[1] // COLORS
    half = third // 2
    for c in range(COLORS):
        bit = sc[S_BITS + ORDER[c][0]]
        for at, (ref, pick) in enumerate(((sends[c], 1 - bit), (keeps[c], bit))):
            src = buf.at[u, pl.ds(pl.multiple_of(c * third + pick * half, half), half), :]
            copies.append(pltpu.make_async_copy(src, ref.at[pl.ds(u * half, half), :], sems.at[u, 2 * c + at]))
    start(copies)
    return copies


def wgrad_body(sc, act_h, send_h, peer_h, hlc, hlcp, dup_h, dupp_h, _, s0, s1, s2, k0, k1, k2,
               act, actp, dffn, low, lowp, dup, dupp, buf, sem_in, sem_out):
    side = act.shape[1]
    width = dffn.shape[1]
    loads = [
        pltpu.make_async_copy(act_h, act, sem_in.at[0]),
        pltpu.make_async_copy(send_h.at[:, pl.ds(side, width)], dffn, sem_in.at[1]),
        pltpu.make_async_copy(peer_h, actp, sem_in.at[2]),
        pltpu.make_async_copy(hlc.at[:, pl.ds(0, width)], low, sem_in.at[3]),
        pltpu.make_async_copy(dup_h, dup, sem_in.at[4]),
        pltpu.make_async_copy(hlcp.at[:, pl.ds(0, width)], lowp, sem_in.at[5]),
        pltpu.make_async_copy(dupp_h, dupp, sem_in.at[6]),
    ]
    start(loads)
    sends, keeps = (s0, s1, s2), (k0, k1, k2)
    copies = []
    wait(loads[:3])
    for u in range(2):
        at = slice(u * width, (u + 1) * width)
        val = dot_tn(act[:, at], dffn[...]) + dot_tn(actp[:, at], actp[:, side:])
        buf[u] = val.astype(BF)
        copies += cut_out(sc, buf, u, sends, keeps, sem_out)
    wait(loads[3:])
    for u in range(2):
        at = slice(u * width, (u + 1) * width)
        val = dot_tn(low[...], dup[:, at]) + dot_tn(lowp[...], dupp[:, at])
        buf[2 + u] = val.astype(BF)
        copies += cut_out(sc, buf, 2 + u, sends, keeps, sem_out)
    wait(copies)


def wgrad(sc, act, send, peer, hlc, hlcp, dup, dupp, dep):
    rows, side = act.shape
    width = hlc.shape[1] // 3
    units = 4
    half = width // COLORS // 2
    anywhere = pl.BlockSpec(memory_space=pl.ANY)
    part = shape_of((units * half, width), BF)
    return pl.pallas_call(
        wgrad_body,
        in_specs=[pl.BlockSpec(memory_space=pltpu.SMEM)] + [anywhere] * 8,
        out_specs=[anywhere] * 6,
        out_shape=[part] * 6,
        scratch_shapes=[pltpu.VMEM((rows, side), BF), pltpu.VMEM((rows, side + width), BF), pltpu.VMEM((rows, width), BF),
                        pltpu.VMEM((rows, width), BF), pltpu.VMEM((rows, width), BF), pltpu.VMEM((rows, side), BF),
                        pltpu.VMEM((rows, side), BF), pltpu.VMEM((units, width, width), BF),
                        pltpu.SemaphoreType.DMA((7,)), pltpu.SemaphoreType.DMA((units, 6))],
        compiler_params=params(),
        cost_estimate=cost(16 * rows * width * width, 26 * rows * width),
        name="wgrad",
    )(sc, act, send, peer, hlc, hlcp, dup, dupp, dep)


def wgrad_mix_body(sc, hlc, hlcp, dq_h, dk_h, dv_h, da_h, p1_h, p2_h, terms, small, _, s0, s1, s2, k0, k1, k2, small_o,
                   l1, l1p, l2, l2p, r1, r1p, r2, r2p, buf, sem_in, sem_out):
    width = l1.shape[1]
    core = sc[S_CORE]
    second = pl.ds(pl.multiple_of((1 + core) * width, width), width)
    loads = [
        pltpu.make_async_copy(hlc.at[:, pl.ds(width, width)], l1, sem_in.at[0]),
        pltpu.make_async_copy(hlcp.at[:, pl.ds(width, width)], l1p, sem_in.at[1]),
        pltpu.make_async_copy(p1_h, r1p, sem_in.at[2]),
        pltpu.make_async_copy(hlc.at[:, second], l2, sem_in.at[3]),
        pltpu.make_async_copy(hlcp.at[:, second], l2p, sem_in.at[4]),
        pltpu.make_async_copy(p2_h, r2p, sem_in.at[5]),
    ]
    start(loads)

    @pl.when(core == 0)
    def _():
        start([pltpu.make_async_copy(dq_h, r1, sem_in.at[6]), pltpu.make_async_copy(dk_h, r2, sem_in.at[7])])

    @pl.when(core != 0)
    def _():
        start([pltpu.make_async_copy(dv_h, r1, sem_in.at[6]), pltpu.make_async_copy(da_h, r2, sem_in.at[7])])

    tail = [pltpu.make_async_copy(dq_h, r1, sem_in.at[6]), pltpu.make_async_copy(dk_h, r2, sem_in.at[7])]
    small_o[...] = small[...] + (terms[0:16, :].astype(F32) + terms[16:32, :].astype(F32))
    sends, keeps = (s0, s1, s2), (k0, k1, k2)
    wait(loads[:3] + tail[:1])
    buf[0] = (dot_tn(l1[...], r1[...]) + dot_tn(l1p[...], r1p[...])).astype(BF)
    copies = cut_out(sc, buf, 0, sends, keeps, sem_out)
    wait(loads[3:] + tail[1:])
    buf[1] = (dot_tn(l2[...], r2[...]) + dot_tn(l2p[...], r2p[...])).astype(BF)
    copies += cut_out(sc, buf, 1, sends, keeps, sem_out)
    wait(copies)


def wgrad_mix(sc, hlc, hlcp, dq, dk, dv, da, p1, p2, terms, small, dep):
    rows, width = dq.shape
    units = 2
    half = width // COLORS // 2
    anywhere = pl.BlockSpec(memory_space=pl.ANY)
    vmem = pl.BlockSpec(memory_space=pltpu.VMEM)
    part = shape_of((units * half, width), BF)
    return pl.pallas_call(
        wgrad_mix_body,
        in_specs=[pl.BlockSpec(memory_space=pltpu.SMEM)] + [anywhere] * 8 + [vmem] * 2 + [anywhere],
        out_specs=[anywhere] * 6 + [vmem],
        out_shape=[part] * 6 + [shape_of(small.shape, F32)],
        scratch_shapes=[pltpu.VMEM((rows, width), BF)] * 8 + [pltpu.VMEM((units, width, width), BF),
                        pltpu.SemaphoreType.DMA((8,)), pltpu.SemaphoreType.DMA((units, 6))],
        compiler_params=params(),
        cost_estimate=cost(8 * rows * width * width, 20 * rows * width),
        name="wgrad_mix",
    )(sc, hlc, hlcp, dq, dk, dv, da, p1, p2, terms, small, dep)


def add_rows(one, two):
    return (one.astype(F32) + two.astype(F32)).astype(BF)


def fold_body(sc, *refs, units, stage, small, deps):
    keeps, gots = refs[:COLORS], refs[COLORS:2 * COLORS]
    outs = refs[2 * COLORS + small + deps:]
    rows = keeps[0].shape[0] // units
    half = rows // 2
    merged = stage == 2
    for c in range(COLORS):
        bit = sc[S_BITS + (3 if merged else ORDER[c][stage + 1])]
        for u in range(units):
            go = pl.ds(pl.multiple_of(u * rows + (1 - bit) * half, LEAF), half)
            stay = pl.ds(pl.multiple_of(u * rows + bit * half, LEAF), half)
            send, keep = (outs[0], outs[1]) if merged else (outs[c], outs[COLORS + c])
            at = (c * units + u) * half if merged else u * half
            send[at:at + half, :] = add_rows(keeps[c][go, :], gots[c][go, :])
            keep[at:at + half, :] = add_rows(keeps[c][stay, :], gots[c][stay, :])
    if small:
        old, new, send = refs[2 * COLORS], outs[-1], outs[0]
        low = units * rows
        val = old[...] + (gots[0][low:low + 16, :].astype(F32) + gots[0][low + 16:low + 32, :].astype(F32))
        new[...] = val
        high, rest = split_terms(val)
        at = send.shape[0] - 32
        send[at:at + 16, :] = high
        send[at + 16:at + 32, :] = rest


def fold(sc, keeps, gots, small, units, stage, deps=()):
    rows, width = keeps[0].shape
    vmem = pl.BlockSpec(memory_space=pltpu.VMEM)
    has = small is not None
    extra = 32 if has else 0
    if stage == 2:
        outs = [shape_of((COLORS * rows // 2 + extra, width), BF), shape_of((COLORS * rows // 2, width), BF)]
    else:
        outs = [shape_of((rows // 2 + (extra if c == 0 else 0), width), BF) for c in range(COLORS)]
        outs += [shape_of((rows // 2, width), BF)] * COLORS
    args = list(keeps) + list(gots)
    if has:
        args.append(small)
        outs.append(shape_of(small.shape, F32))
    got = pl.pallas_call(
        functools.partial(fold_body, units=units, stage=stage, small=has, deps=len(deps)),
        out_shape=outs,
        in_specs=[pl.BlockSpec(memory_space=pltpu.SMEM)] + [vmem] * len(args) + [pl.BlockSpec(memory_space=pl.ANY)] * len(deps),
        out_specs=[vmem] * len(outs),
        compiler_params=params(),
        cost_estimate=cost(6 * rows * width, 18 * rows * width),
        name="fold",
    )(sc, *args, *deps)
    if has:
        small = got[-1]
    if stage == 2:
        return [got[0]], [got[1]], small
    return got[:COLORS], got[COLORS:2 * COLORS], small


def total_body(keep, got, *refs, small):
    rows = keep.shape[0]
    out = refs[-2] if small else refs[-1]
    out[...] = add_rows(keep[...], got[0:rows, :])
    if small:
        refs[-1][...] = refs[0][...] + (
            got[rows:rows + 16, :].astype(F32) + got[rows + 16:rows + 32, :].astype(F32))


def total(keep, got, small, deps):
    vmem = pl.BlockSpec(memory_space=pltpu.VMEM)
    args = [keep, got]
    outs = [shape_of(keep.shape, BF)]
    if small is not None:
        args.append(small)
        outs.append(shape_of(small.shape, F32))
    res = pl.pallas_call(
        functools.partial(total_body, small=small is not None),
        out_shape=outs,
        in_specs=[vmem] * len(args) + [pl.BlockSpec(memory_space=pl.ANY)] * len(deps),
        out_specs=[vmem] * len(outs),
        compiler_params=params(),
        cost_estimate=cost(keep.size, 6 * keep.size),
        name="total",
    )(*args, *deps)
    return res[0], (res[1] if small is not None else None)


def join_body(sc, *refs, units, stage, deps):
    outs = refs[-COLORS:]
    n = (len(refs) - COLORS - deps) // 2
    owns, gots = refs[:n], refs[n:2 * n]
    rows = outs[0].shape[0] // units
    half = rows // 2
    for c in range(COLORS):
        bit = sc[S_BITS + (3 if stage == 3 else ORDER[c][stage])]
        own, got = (owns[0], gots[0]) if n == 1 else (owns[c], gots[c])
        for u in range(units):
            at = (c * units + u) * half if n == 1 else u * half
            outs[c][pl.ds(pl.multiple_of(u * rows + bit * half, LEAF), half), :] = own[at:at + half, :]
            outs[c][pl.ds(pl.multiple_of(u * rows + (1 - bit) * half, LEAF), half), :] = got[at:at + half, :]


def joined(sc, owns, gots, units, stage, deps=()):
    width = owns[0].shape[1]
    rows = 2 * owns[0].shape[0] // (COLORS if len(owns) == 1 else 1)
    vmem = pl.BlockSpec(memory_space=pltpu.VMEM)
    args = list(owns) + list(gots)
    return pl.pallas_call(
        functools.partial(join_body, units=units, stage=stage, deps=len(deps)),
        out_shape=[shape_of((rows, width), BF)] * COLORS,
        in_specs=[pl.BlockSpec(memory_space=pltpu.SMEM)] + [vmem] * len(args)
        + [pl.BlockSpec(memory_space=pl.ANY)] * len(deps),
        out_specs=[vmem] * COLORS,
        compiler_params=params(),
        cost_estimate=cost(rows * width, 12 * rows * width),
        name="join",
    )(sc, *args, *deps)


def pack_body(*refs, deps):
    out = refs[-1]
    rows = refs[0].shape[0]
    for c in range(COLORS):
        out[c * rows:(c + 1) * rows, :] = refs[c][...]


def pack(values, deps):
    rows, width = values[0].shape
    vmem = pl.BlockSpec(memory_space=pltpu.VMEM)
    return pl.pallas_call(
        functools.partial(pack_body, deps=len(deps)),
        out_shape=shape_of((COLORS * rows, width), BF),
        in_specs=[vmem] * COLORS + [pl.BlockSpec(memory_space=pl.ANY)] * len(deps),
        out_specs=vmem,
        compiler_params=params(),
        cost_estimate=cost(rows * width, 12 * rows * width),
        name="pack",
    )(*values, *deps)


def final_body(sc, *refs, mixed):
    j = pl.program_id(0)
    ins, outs = refs[:4 * COLORS], refs[4 * COLORS:]
    third = outs[0].shape[0] // COLORS
    half = third // 2

    def write(out, owns, gots):
        for c in range(COLORS):
            bit = sc[S_BITS + ORDER[c][0]]
            out[pl.ds(pl.multiple_of(c * third + bit * half, half), half), :] = owns[c][...].astype(F32)
            out[pl.ds(pl.multiple_of(c * third + (1 - bit) * half, half), half), :] = gots[c][...].astype(F32)

    for side in range(2):
        owns = ins[2 * side * COLORS:(2 * side + 1) * COLORS]
        gots = ins[(2 * side + 1) * COLORS:(2 * side + 2) * COLORS]
        here = (j >= 2) if side else (j < 2)
        if not mixed:
            @pl.when(here)
            def _():
                write(outs[0], owns, gots)
        else:
            other = (j % 2 == 1) & ((sc[S_CORE] == 0) if side else (sc[S_CORE] != 0))

            @pl.when(here & jnp.logical_not(other))
            def _():
                write(outs[0], owns, gots)

            @pl.when(here & other)
            def _():
                write(outs[1], owns, gots)


def final(sc, mine, theirs, first, kind, packed):
    width = mine[0].shape[1]
    half = width // COLORS // 2
    own = pl.BlockSpec((half, width), lambda j, s: (first + jnp.minimum(j, 1), 0))
    far = pl.BlockSpec((half, width), lambda j, s: (first + jnp.maximum(j - 2, 0), 0))

    units = packed.shape[0] // (COLORS * half)

    def far_got(c):
        return pl.BlockSpec((half, width), lambda j, s: (c * units + first + jnp.maximum(j - 2, 0), 0))

    def place(j, s):
        return jnp.where(j < 2, s[S_CORE], 1 - s[S_CORE]) * 2 + j % 2

    if kind == "rows":
        specs = [pl.BlockSpec((width, width), lambda j, s: (place(j, s), 0))]
        outs = [shape_of((4 * width, width), F32)]
    elif kind == "cols":
        specs = [pl.BlockSpec((width, width), lambda j, s: (0, place(j, s)))]
        outs = [shape_of((width, 4 * width), F32)]
    else:
        specs = [pl.BlockSpec((width, width), lambda j, s: (0, jnp.minimum(place(j, s), 2))), full((width, width))]
        outs = [shape_of((width, 3 * width), F32), shape_of((width, width), F32)]
    grid = pltpu.PrefetchScalarGridSpec(
        num_scalar_prefetch=1,
        grid=(4,),
        in_specs=[own] * (2 * COLORS) + [far] * COLORS + [far_got(c) for c in range(COLORS)],
        out_specs=specs,
    )
    return pl.pallas_call(
        functools.partial(final_body, mixed=len(outs) == 2),
        grid_spec=grid,
        out_shape=outs,
        compiler_params=params(),
        cost_estimate=cost(4 * width * width, 24 * width * width),
        name="final",
    )(sc, *mine, *theirs, *([packed] * COLORS))


def body(
    hidden_in,
    lengths,
    qkv_weight,
    query_bias,
    value_bias,
    out_weight,
    out_bias,
    attn_gain,
    attn_shift,
    up_weight,
    up_bias,
    down_weight,
    down_bias,
    ffn_gain,
    ffn_shift,
    cotangent,
):
    count, local, width = hidden_in.shape
    nseq = lax.axis_size("seq")
    ndp = lax.axis_size("dp")
    seq = lax.axis_index("seq")
    dp = lax.axis_index("dp")
    core = dp & 1
    flat = seq * ndp + dp
    members = nseq * ndp
    line = lambda vec: vec.reshape(1, -1)

    axes = [ndp, 2 * ndp]
    mask = 2
    while mask < ndp:
        axes.append(mask)
        mask *= 2
    later = axes[4:]

    def permute(value, mask):
        return lax.ppermute(value, ("seq", "dp"), [(i, i ^ mask) for i in range(members)])

    def over(values, stage):
        if stage == 3:
            return [permute(values[0], axes[3])]
        return [permute(values[c], axes[ORDER[c][stage]]) for c in range(COLORS)]

    def core_swap(value):
        return permute(value, 1)

    holder = jnp.minimum(seq, count - 1)
    own_len = lax.dynamic_index_in_dim(lengths, holder, 0, False)
    own_len = jnp.where(seq < count, own_len, nseq * local)
    bits = [jnp.where((flat & mask) != 0, 1, 0) for mask in axes[:4]]
    sc = jnp.stack([seq, own_len, core] + bits + [core]).astype(jnp.int32)

    def to_holder(value):
        blocks = [lax.dynamic_index_in_dim(value, holder, 0, False)]
        parts = [lax.dynamic_index_in_dim(value, jnp.minimum(seq ^ k, count - 1), 0, False) for k in range(1, nseq)]
        for k in range(1, nseq):
            pairs = [(i, i ^ k) for i in range(nseq) if (i ^ k) < count]
            blocks.append(lax.ppermute(parts[k - 1], "seq", pairs))
        return blocks

    hids = to_holder(hidden_in)
    *hids, cot_in = lax.optimization_barrier(tuple(hids) + (cotangent,))
    cots = to_holder(cot_in)
    cots[0] = jnp.where(seq < count, cots[0], jnp.zeros_like(cots[0]))

    hlc, q, k, v, lse, n1, r1 = attn_fwd(
        sc, hids, qkv_weight, line(query_bias), line(value_bias), out_weight, line(out_bias),
        line(attn_gain), line(attn_shift))
    hlc_p = core_swap(hlc)
    act, send, dup, dup_send, lo, dres, dattn, dctx, stat = ffn(
        sc, hlc, n1, r1, up_weight, down_weight, out_weight, cots, line(attn_gain), line(attn_shift),
        line(up_bias), line(down_bias), line(ffn_gain), line(ffn_shift))
    send_p = core_swap(send)
    dup_p = core_swap(dup_send)
    *part, base = attn_bwd(sc, q, k, v, dctx, lse, qkv_weight, dres, dattn, stat, lo, ())
    got = wgrad(sc, act, send, send_p, hlc, hlc_p, dup, dup_p, base)
    sends1, keeps1 = got[:COLORS], got[COLORS:]
    gots1 = over(sends1, 0)
    dq, dk, dv, one, two, small, terms, i0, i1, i2, i3 = attn_bwd(
        sc, q, k, v, dctx, lse, qkv_weight, base, dattn, part[5], lo, tuple(part[:5]), (keeps1[0],))
    one_p, two_p, terms_p = core_swap(one), core_swap(two), core_swap(terms)
    sends1, keeps1, _ = fold(sc, keeps1, gots1, None, 4, 0, (terms,))
    gots1 = over(sends1, 1)
    *got, small = wgrad_mix(sc, hlc, hlc_p, dq, dk, dv, dattn, one_p, two_p, terms_p, small, keeps1[0])
    sends2, keeps2 = list(got[:COLORS]), got[COLORS:]
    high, rest = split_terms(small)
    sends2[0] = jnp.concatenate([sends2[0], high, rest], 0)
    gots2 = over(sends2, 0)
    token = keeps2[0]

    def step(kind, token, keeps, gots, small, units, stage):
        if kind == "fold":
            if stage < 3:
                sends, keeps, small = fold(sc, keeps, gots, small, units, stage, (token,))
            else:
                whole, small = total(keeps[0], gots[0], small, (token,))
                for mask in later:
                    if small is None:
                        whole = add_rows(whole, permute(whole, mask))
                    else:
                        high, rest = split_terms(small)
                        more = permute(jnp.concatenate([whole, high, rest], 0), mask)
                        size = whole.shape[0]
                        whole = add_rows(whole, more[:size])
                        small = small + (more[size:size + 16].astype(F32) + more[size + 16:].astype(F32))
                sends = keeps = [whole]
        else:
            deps = (token,) + (tuple(back[1:]) if (units, stage) == (4, 3) else ())
            sends = keeps = joined(sc, keeps, gots, units, stage, deps)
        return sends, keeps, small, keeps[0]

    plan = [("fold", 1, 1), ("fold", 2, 0), ("fold", 1, 2), ("fold", 2, 1), ("fold", 1, 3), ("fold", 2, 2),
            ("join", 1, 3), ("fold", 2, 3), ("join", 1, 2), ("join", 2, 3), ("join", 1, 1), ("join", 2, 2),
            ("join", 2, 1)]
    state = {1: (keeps1, gots1, None, 4), 2: (keeps2, gots2, small, 2)}
    far = {}
    for at, (kind, piece, stage) in enumerate(plan):
        keeps, gots, small, units = state[piece]
        sends, keeps, small, token = step(kind, token, keeps, gots, small, units, stage)
        if kind == "fold":
            upcoming = stage + 1 if stage < 3 else 3
        else:
            upcoming = stage - 1
        gots = over(sends, upcoming)
        state[piece] = (keeps, gots, small, units)
        if kind == "join" and stage == 1:
            far[piece] = [core_swap(value) for value in keeps]
        if at == 0:
            blocks = [i0, i1, i2, i3]
            back = [i0]
            for k_at in range(1, nseq):
                pairs = [(i, i ^ k_at) for i in range(nseq) if i < count]
                back.append(lax.ppermute(blocks[k_at], "seq", pairs))

    keeps1, gots1 = state[1][:2]
    packed1 = core_swap(pack(gots1, (token,)))
    shown = []
    for p in range(count):
        value = back[0]
        for k_at in range(1, nseq):
            value = jnp.where((seq ^ p) == k_at, back[k_at], value)
        shown.append(value)
    layer_out = jnp.stack([value[:local] for value in shown])
    input_grad = jnp.stack([value[local:] for value in shown])
    mine1 = list(keeps1) + list(gots1)
    (down_grad,) = final(sc, mine1, far[1], 0, "rows", packed1)
    (up_grad,) = final(sc, mine1, far[1], 2, "cols", packed1)
    keeps2, gots2, small, _ = state[2]
    packed2 = core_swap(pack(gots2, (down_grad, up_grad)))
    qkv_grad, out_grad = final(sc, list(keeps2) + list(gots2), far[2], 0, "mixed", packed2)
    return (
        layer_out,
        input_grad,
        qkv_grad,
        small[6],
        small[7],
        out_grad,
        small[5],
        small[3],
        small[4],
        up_grad,
        small[8:12].reshape(-1),
        down_grad,
        small[2],
        small[0],
        small[1],
    )


def solution(mesh):
    split = P("dp", "seq", None)
    return jax.shard_map(
        body,
        mesh=mesh,
        in_specs=(split, P("dp")) + (P(),) * 13 + (split,),
        out_specs=(split, split) + (P(),) * 13,
        check_vma=False,
    )
```
